512 devices in a mesh: shot: 32 (over z_hi, y, core), tx: 4 (over x), ty: 4 (over z_lo).
Axes of the slice: x: 4, y: 8, z: 8 (z_hi: 2, z_lo: 4; z = z_hi * 4 + z_lo), core: 2. Of those that a mesh axis runs over, the one named last changes fastest.
Arguments:
- wave_now: float32 [128, 64, 64, 128], P('shot', 'tx', 'ty'), may hold values from -6 to 6
- wave_prev: float32 [128, 64, 64, 128], P('shot', 'tx', 'ty'), may hold values from -6 to 6
- courant: float32 [64, 64, 128], P('tx', 'ty'), may hold values from 0.02 to 0.3
- rec_index: int32 [4, 4, 512], P('tx', 'ty'), may hold values from 0 to 32767
- rec_history: bfloat16 [128, 8, 4, 4, 512], P('shot', None, 'tx', 'ty'), may hold values from -6 to 6
- green: bfloat16 [2, 8192, 8192], P(None, ('tx', 'ty'), 'shot'), may hold values from -0.046875 to 0.046875
- lag_delay: int32 [2], replicated, may hold values from 1 to 8, as said below
- emit_cells: int32 [4, 4, 8, 512], P('tx', 'ty'), may hold values from 0 to 32767
- emit_weights: float32 [4, 4, 8, 512], P('tx', 'ty'), may hold values from 0.25 to 1
Outputs:
- wave_out: float32 [128, 64, 64, 128], P('shot', 'tx', 'ty')
- wave_last: float32 [128, 64, 64, 128], P('shot', 'tx', 'ty')
- emission: float32 [128, 8, 4, 4, 512], P('shot', None, 'tx', 'ty')
The draws below stay inside these ranges and needn't reach their ends.
Inputs may be any that keep to these rules, and one draw needn't show every extreme that they name: `lag_delay`: one lag group has delay 8, the other a smaller one.
All inputs are finite; a program needn't handle non-finite values.
Results may differ from the reference program's by a relative error of at most 0.0023.
Values may be sent and summed in bfloat16 or wider, within the bound.
No kernel may reach another device: no remote copies, remote signals or barrier semaphores. Data moves between devices by JAX's collectives and lax.ppermute only.
A program may use at most 128 MiB of HBM per device.

```python
import math
import jax
import jax.numpy as jnp
from jax import lax

CX = 16
CY = 16
CZ = 128
STEPS = 8
HIST = 8
LAGS = 2
REC_TILE = 512
EMIT_TILE = 512
RECS = 8192
EMITS = 8192
SHOTS = 128
NX = 64
NY = 64
N_SHOT = 32
N_TX = 4
N_TY = 4


def draw_lag_delay(key, part):
    subkeys = jax.random.split(jax.random.fold_in(key, 11))
    other = jax.random.randint(subkeys[0], (), 1, HIST)
    flipped = jax.random.randint(subkeys[1], (), 0, 2)
    first = jnp.where(flipped == 0, HIST, other)
    second = jnp.where(flipped == 0, other, HIST)
    return jnp.stack([first, second]).astype(jnp.int32)


def plant(drawn, stream_key, low, high):
    spot = [jax.random.randint(jax.random.fold_in(stream_key, axis), (), 0, length) for axis, length in enumerate(drawn.shape)]
    widest = drawn.shape.index(max(drawn.shape))
    next_to = spot[:widest] + [(spot[widest] + 1) % drawn.shape[widest]] + spot[widest + 1:]
    return drawn.at[tuple(spot)].set(low).at[tuple(next_to)].set(high)


def block_levels(rng, shape, pieces, low, top_value):
    def one(position, parts):
        heights = jax.random.uniform(jax.random.fold_in(jax.random.fold_in(rng, 6), position), (parts,), jnp.float32, low / len(pieces), top_value / len(pieces))
        return jnp.repeat(jnp.exp(heights), shape[position] // parts).reshape((-1,) + (1,) * (len(shape) - position - 1))

    loudness = one(*pieces[0])
    for cut in pieces[1:]:
        loudness = loudness * one(*cut)
    return loudness


def noise(own_key, dims, spread, most, cuts=(), kind=jnp.bfloat16):
    entries = jax.random.normal(own_key, dims, jnp.float32) * spread
    if len(cuts) > 0:
        entries = block_levels(own_key, dims, cuts, -0.22, 0.18) * entries
    return jnp.clip(entries, min=-most, max=most).astype(kind)


def setup_inputs(seed: int = 0) -> dict:
    key_list = jax.random.split(jax.random.key(seed), 10)
    wave_now = noise(key_list[0], (SHOTS, NX, NY, CZ), 1.0, 6.0, ((0, 32), (1, 4), (2, 4)), jnp.float32)
    wave_prev = noise(key_list[1], (SHOTS, NX, NY, CZ), 1.0, 6.0, ((0, 32), (1, 4), (2, 4)), jnp.float32)
    courant = jnp.clip(jnp.exp(math.log(0.3) - 2.7080503 * jax.random.uniform(key_list[2], (NX, NY, CZ), jnp.float32) ** block_levels(key_list[2], (NX, NY, CZ), ((0, 4), (1, 4)), -0.2, 0.2)), 0.02, 0.3)
    rec_index = plant(jax.random.randint(key_list[3], (N_TX, N_TY, REC_TILE), 0, CX * CY * CZ), jax.random.fold_in(key_list[3], 1), 0, (CX * CY * CZ) - 1).astype(jnp.int32)
    rec_history = noise(key_list[4], (SHOTS, HIST, N_TX, N_TY, REC_TILE), 1.0, 6.0, ((0, 32), (2, 4), (3, 4)))
    green = noise(key_list[5], (LAGS, RECS, EMITS), (LAGS * RECS) ** -0.5, 0.046875, ((1, 16), (2, 32)))
    lag_delay = draw_lag_delay(jax.random.fold_in(key_list[9], 71), 0)
    emit_cells = plant(jax.random.randint(key_list[7], (N_TX, N_TY, 8, EMIT_TILE), 0, CX * CY * CZ), jax.random.fold_in(key_list[7], 1), 0, (CX * CY * CZ) - 1).astype(jnp.int32)
    emit_weights = jnp.clip(0.25 + 0.75 * jax.random.uniform(key_list[8], (N_TX, N_TY, 8, EMIT_TILE), jnp.float32) ** block_levels(key_list[8], (N_TX, N_TY, 8, EMIT_TILE), ((0, 4), (1, 4)), -0.2, 0.2), 0.25, 1.0)
    return {"wave_now": wave_now, "wave_prev": wave_prev, "courant": courant, "rec_index": rec_index, "rec_history": rec_history, "green": green, "lag_delay": lag_delay, "emit_cells": emit_cells, "emit_weights": emit_weights}


def laplace(field):
    padded = jnp.pad(field, ((0, 0), (1, 1), (1, 1), (1, 1)))
    centre = padded[:, 1:-1, 1:-1, 1:-1]
    total = padded[:, 2:, 1:-1, 1:-1] + padded[:, :-2, 1:-1, 1:-1]
    total = total + padded[:, 1:-1, 2:, 1:-1] + padded[:, 1:-1, :-2, 1:-1]
    total = total + padded[:, 1:-1, 1:-1, 2:] + padded[:, 1:-1, 1:-1, :-2]
    return total - 6.0 * centre


def tiles_view(field):
    shots_all = field.shape[0]
    viewed = field.reshape(shots_all, N_TX, CX, N_TY, CY, CZ).transpose(0, 1, 3, 2, 4, 5)
    return viewed.reshape(shots_all, N_TX, N_TY, CX * CY * CZ)


def reference(wave_now, wave_prev, courant, rec_index, rec_history, green, lag_delay, emit_cells, emit_weights):
    shots_all = wave_now.shape[0]
    current, previous = wave_now, wave_prev
    traces = []
    index_full = jnp.broadcast_to(rec_index[None], (shots_all,) + rec_index.shape)
    for step in range(STEPS):
        following = 2.0 * current - previous + courant[None] * laplace(current)
        previous, current = current, following
        sampled = jnp.take_along_axis(tiles_view(current), index_full, axis=3)
        traces.append(sampled.astype(jnp.bfloat16))
    new_records = jnp.stack(traces, 1)
    full = jnp.concatenate([rec_history, new_records], 1).reshape(shots_all, HIST + STEPS, RECS)
    columns = jnp.zeros((shots_all * STEPS, EMITS), jnp.float32)
    for lag_group in range(LAGS):
        offset = (HIST - lag_delay[lag_group]).astype(jnp.int32)
        window = lax.dynamic_slice_in_dim(full, offset, STEPS, 1).reshape(shots_all * STEPS, RECS)
        columns = columns + jnp.dot(window, green[lag_group], preferred_element_type=jnp.float32)
    columns = columns.reshape(shots_all, STEPS, N_SHOT, N_TX * N_TY, EMIT_TILE // N_SHOT)
    emission = columns.transpose(0, 1, 3, 2, 4).reshape(shots_all, STEPS, N_TX, N_TY, EMIT_TILE)
    last = emission[:, STEPS - 1]
    values = emit_weights[None] * last[:, :, :, None, :]
    shot_idx = jnp.arange(shots_all)[:, None, None, None, None]
    tile_a = jnp.arange(N_TX)[None, :, None, None, None]
    tile_b = jnp.arange(N_TY)[None, None, :, None, None]
    viewed = tiles_view(current).at[shot_idx, tile_a, tile_b, emit_cells[None]].add(values)
    wave_out = viewed.reshape(shots_all, N_TX, N_TY, CX, CY, CZ).transpose(0, 1, 3, 2, 4, 5)
    wave_out = wave_out.reshape(shots_all, N_TX * CX, N_TY * CY, CZ)
    return wave_out, previous, emission
```

```python
import jax
import jax.numpy as jnp
from jax import lax
from jax.experimental import pallas as pl
from jax.experimental.pallas import tpu as pltpu
from jax.sharding import PartitionSpec as P

STEPS = 8
HIST = 8
BAND = 8
TILE = 16
WIDE = TILE + 2 * BAND
DEPTH = 128
PAD = 8
F32 = jnp.float32
BF16 = jnp.bfloat16
NT = (((1,), (1,)), ((), ()))


def shot_id(half, row, core):
    return (half * 8 + row) * 2 + core


SHOT_COORDS = [(h, r, c) for h in range(2) for r in range(8) for c in range(2)]
CORE_SWAP = [(shot_id(h, r, c), shot_id(h, r, 1 - c)) for h, r, c in SHOT_COORDS]
HALF_SWAP = [(shot_id(h, r, c), shot_id(1 - h, r, c)) for h, r, c in SHOT_COORDS]
ROW_GROUPS = [[shot_id(h, r, c) for r in range(8)] for h in range(2) for c in range(2)]
UP = [(i, i + 1) for i in range(3)]
DOWN = [(i + 1, i) for i in range(3)]


def row_exchange(x):
    return lax.all_to_all(
        x, "shot", split_axis=0, concat_axis=0, tiled=True, axis_index_groups=ROW_GROUPS
    )


def spread_rows(x):
    return row_exchange(jnp.broadcast_to(x[None], (8, *x.shape)))


def stencil_kernel(
    now, prev, speed_in, xm, xp, ym, yp, cmm, cmp, cpm, cpp, rows_hot, lanes_hot,
    next_out, last_out, rec_out, cur, prv, spd, sems, out_sems,
):
    shots = now.shape[0]
    low = slice(0, BAND)
    mid = slice(BAND, BAND + TILE)
    high = slice(BAND + TILE, WIDE)
    ylow = slice(PAD, PAD + BAND)
    ymid = slice(PAD + BAND, PAD + BAND + TILE)
    yhigh = slice(PAD + BAND + TILE, PAD + WIDE)
    copies = []

    def add(src, dst):
        copies.append(pltpu.make_async_copy(src, dst, sems.at[len(copies)]))

    add(now, cur.at[:, mid, ymid])
    add(prev, prv.at[:, mid, ymid])
    add(speed_in, spd.at[mid, ymid])
    for block, xs, ys in (
        (xm, low, ymid), (xp, high, ymid), (ym, mid, ylow), (yp, mid, yhigh),
        (cmm, low, ylow), (cmp, low, yhigh), (cpm, high, ylow), (cpp, high, yhigh),
    ):
        add(block.at[pl.ds(0, shots)], cur.at[:, xs, ys])
        add(block.at[pl.ds(shots, shots)], prv.at[:, xs, ys])
        add(block.at[2 * shots], spd.at[xs, ys])
    for copy in copies:
        copy.start()
    for copy in copies:
        copy.wait()

    bufs = (cur, prv)
    lanes = lax.broadcasted_iota(jnp.int32, (WIDE, DEPTH), 1)
    sel_row = lax.broadcasted_iota(jnp.int32, (shots * STEPS, shots * DEPTH), 0)
    sel_col = lax.broadcasted_iota(jnp.int32, (shots * STEPS, shots * DEPTH), 1)
    records = jnp.zeros((shots * STEPS, rows_hot.shape[0]), F32)
    for step in range(1, STEPS + 1):
        src, dst = bufs[(step - 1) % 2], bufs[step % 2]
        if step < STEPS:
            start, count = PAD, WIDE
        else:
            start, count = PAD + BAND, TILE
        lane = lanes[:count]

        def body(x, carry, src=src, dst=dst, start=start, count=count, lane=lane):
            speed = spd[x, pl.ds(start, count), :]
            centre = 2.0 - 6.0 * speed
            for s in range(shots):
                u = src[s, x, pl.ds(start, count), :]
                total = src[s, x - 1, pl.ds(start, count), :] + src[s, x + 1, pl.ds(start, count), :]
                total = total + src[s, x, pl.ds(start - 1, count), :]
                total = total + src[s, x, pl.ds(start + 1, count), :]
                total = total + jnp.where(lane > 0, pltpu.roll(u, 1, 1), 0.0)
                total = total + jnp.where(lane < DEPTH - 1, pltpu.roll(u, DEPTH - 1, 1), 0.0)
                dst[s, x, pl.ds(start, count), :] = (
                    centre * u - dst[s, x, pl.ds(start, count), :] + speed * total
                )
            return carry

        lax.fori_loop(step, WIDE - step, body, 0)
        if step < STEPS:
            field = jnp.concatenate(
                [dst[s, mid, ymid, :].reshape(TILE * TILE, DEPTH).astype(BF16) for s in range(shots)],
                axis=1,
            )
            picked = jnp.dot(rows_hot[...], field, preferred_element_type=F32)
            mask = jnp.concatenate([lanes_hot[...]] * shots, axis=1)
            picked = (picked * mask).astype(BF16)
            sel = (sel_row == (sel_col // DEPTH) * STEPS + (step - 1)).astype(F32).astype(BF16)
            records = records + lax.dot_general(sel, picked, NT, preferred_element_type=F32)
    rec_out[...] = records.astype(BF16)
    out_next = pltpu.make_async_copy(bufs[STEPS % 2].at[:, mid, ymid], next_out, out_sems.at[0])
    out_last = pltpu.make_async_copy(bufs[(STEPS - 1) % 2].at[:, mid, ymid], last_out, out_sems.at[1])
    out_next.start()
    out_last.start()
    out_next.wait()
    out_last.wait()


def stencil(now, prev, speed, halos, rows_hot, lanes_hot):
    shots = now.shape[0]
    points = rows_hot.shape[0]
    anywhere = pl.BlockSpec(memory_space=pl.ANY)
    vmem = pl.BlockSpec(memory_space=pltpu.VMEM)
    wide = (shots, WIDE, WIDE + 2 * PAD, DEPTH)
    return pl.pallas_call(
        stencil_kernel,
        out_shape=(
            jax.ShapeDtypeStruct(now.shape, F32),
            jax.ShapeDtypeStruct(now.shape, F32),
            jax.ShapeDtypeStruct((shots * STEPS, points), BF16),
        ),
        in_specs=[anywhere] * 11 + [vmem] * 2,
        out_specs=(anywhere, anywhere, vmem),
        scratch_shapes=[
            pltpu.VMEM(wide, F32),
            pltpu.VMEM(wide, F32),
            pltpu.VMEM(wide[1:], F32),
            pltpu.SemaphoreType.DMA((27,)),
            pltpu.SemaphoreType.DMA((2,)),
        ],
        compiler_params=pltpu.CompilerParams(vmem_limit_bytes=48 << 20),
        cost_estimate=pl.CostEstimate(flops=2_000_000_000, bytes_accessed=12_000_000, transcendentals=0),
        name="stencil",
    )(now, prev, speed, *halos, rows_hot, lanes_hot)


def columns_kernel(delay, old, new, green, out):
    groups, rows, points = old.shape
    half = rows // 2
    lags = green.shape[0]
    width = green.shape[2]
    sel_row = lax.broadcasted_iota(jnp.int32, (half, 2 * rows), 0)
    sel_col = lax.broadcasted_iota(jnp.int32, (half, 2 * rows), 1)
    col_shot = (sel_col % rows) // STEPS
    col_time = (sel_col // rows) * HIST + sel_col % STEPS
    both = [jnp.concatenate([old[g], new[g]], axis=0) for g in range(groups)]
    parts = []
    for h in range(2):
        row_shot = sel_row // STEPS + h * (half // STEPS)
        total = None
        for lag in range(lags):
            wanted = HIST + sel_row % STEPS - delay[lag]
            sel = jnp.logical_and(col_shot == row_shot, col_time == wanted)
            sel = sel.astype(F32).astype(BF16)
            window = jnp.concatenate(
                [jnp.dot(sel, b, preferred_element_type=F32).astype(BF16) for b in both], axis=0
            )
            term = jnp.dot(window, green[lag], preferred_element_type=F32)
            total = term if total is None else total + term
        parts.append(total)
    lane = lax.broadcasted_iota(jnp.int32, (groups * half, 128), 1)
    for m in range(width // 128):
        a = parts[0][:, m * 128 : (m + 1) * 128]
        b = parts[1][:, m * 128 : (m + 1) * 128]
        out[2 * m] = jnp.where(lane < 64, a, pltpu.roll(b, 64, 1))
        out[2 * m + 1] = jnp.where(lane < 64, pltpu.roll(a, 64, 1), b)


def columns(delay, old, new, green):
    vmem = pl.BlockSpec(memory_space=pltpu.VMEM)
    return pl.pallas_call(
        columns_kernel,
        out_shape=jax.ShapeDtypeStruct((16, 128, 128), F32),
        in_specs=[pl.BlockSpec(memory_space=pltpu.SMEM), vmem, vmem, vmem],
        out_specs=vmem,
        compiler_params=pltpu.CompilerParams(vmem_limit_bytes=32 << 20),
        cost_estimate=pl.CostEstimate(flops=1_000_000_000, bytes_accessed=4_000_000, transcendentals=0),
        name="columns",
    )(delay, old, new, green)


def inject_kernel(em, cells, weights, field, wave_out, emission, rhs_high, rhs_low, acc):
    shots = field.shape[0]
    points = cells.shape[1]
    lane = lax.broadcasted_iota(jnp.int32, (16, 128), 1)
    for sh in range(2):
        for tile in range(4):
            z = tile // 2
            block = None
            for i in range(4):
                piece = em[(tile % 2) * 4 + i]
                shift = (i * 32 - sh * 64 - z * 32) % 128
                if shift:
                    piece = pltpu.roll(piece, shift, 1)
                block = piece if block is None else jnp.where(lane >= i * 32, piece, block)
            emission[pl.ds(sh * 16, 16), pl.ds(tile * 128, 128)] = block

    acc[...] = jnp.zeros_like(acc)
    row_iota = lax.broadcasted_iota(jnp.int32, (TILE * TILE, points), 0)
    lane_iota = lax.broadcasted_iota(jnp.int32, (DEPTH, points), 0)

    def body(k, carry):
        cell = cells[pl.ds(k, 1), :]
        weight = weights[pl.ds(k, 1), :]
        rows_hot = (row_iota == lax.shift_right_logical(cell, 7)).astype(F32).astype(BF16)
        lane_hot = lane_iota == jnp.bitwise_and(cell, DEPTH - 1)
        for s in range(shots):
            value = weight * emission[pl.ds(s * STEPS + STEPS - 1, 1), :]
            top = value.astype(BF16).astype(F32)
            rest = value - top
            rhs_high[pl.ds(s * DEPTH, DEPTH), :] = jnp.where(lane_hot, top, 0.0).astype(BF16)
            rhs_low[pl.ds(s * DEPTH, DEPTH), :] = jnp.where(lane_hot, rest, 0.0).astype(BF16)
        acc[...] += lax.dot_general(
            rows_hot, rhs_high[...], NT, preferred_element_type=F32
        ) + lax.dot_general(rows_hot, rhs_low[...], NT, preferred_element_type=F32)
        return carry

    lax.fori_loop(0, cells.shape[0], body, 0)
    for s in range(shots):
        wave_out[s] = field[s] + acc[:, s * DEPTH : (s + 1) * DEPTH].reshape(TILE, TILE, DEPTH)


def inject(em, cells, weights, field):
    shots = field.shape[0]
    points = cells.shape[1]
    vmem = pl.BlockSpec(memory_space=pltpu.VMEM)
    return pl.pallas_call(
        inject_kernel,
        out_shape=(
            jax.ShapeDtypeStruct(field.shape, F32),
            jax.ShapeDtypeStruct((shots * STEPS, points), F32),
        ),
        in_specs=[vmem] * 4,
        out_specs=(vmem, vmem),
        scratch_shapes=[
            pltpu.VMEM((shots * DEPTH, points), BF16),
            pltpu.VMEM((shots * DEPTH, points), BF16),
            pltpu.VMEM((TILE * TILE, shots * DEPTH), F32),
        ],
        compiler_params=pltpu.CompilerParams(vmem_limit_bytes=32 << 20),
        cost_estimate=pl.CostEstimate(flops=4_000_000_000, bytes_accessed=4_000_000, transcendentals=0),
        name="inject",
    )(em, cells, weights, field)


def halo_blocks(now, prev, speed):
    def stacked(xs, ys):
        return jnp.concatenate([now[:, xs, ys], prev[:, xs, ys], speed[None, xs, ys]], 0)

    whole = slice(None)
    head, tail = slice(0, BAND), slice(TILE - BAND, TILE)
    xm = lax.ppermute(stacked(tail, whole), "tx", UP)
    xp = lax.ppermute(stacked(head, whole), "tx", DOWN)
    ym = lax.ppermute(stacked(whole, tail), "ty", UP)
    yp = lax.ppermute(stacked(whole, head), "ty", DOWN)
    cmm = lax.ppermute(ym[:, tail], "tx", UP)
    cpp = lax.ppermute(yp[:, head], "tx", DOWN)
    cpm = lax.ppermute(xp[:, :, tail], "ty", UP)
    cmp = lax.ppermute(xm[:, :, head], "ty", DOWN)
    return xm, xp, ym, yp, cmm, cmp, cpm, cpp


def gathered_green(green):
    other = lax.ppermute(green, "shot", HALF_SWAP)
    mine = jnp.concatenate([green, other], -1)
    theirs = lax.ppermute(mine, "shot", CORE_SWAP)
    blocks = jnp.concatenate([mine, theirs], -1)
    width = blocks.shape[-1]
    me = lax.axis_index("shot")
    half, core = me // 16, me % 2
    source = lax.broadcasted_iota(jnp.int32, (width, width), 0)
    target = lax.broadcasted_iota(jnp.int32, (width, width), 1)
    block = source // 256
    place = (
        (source % 256 // 16) * 64
        + jnp.bitwise_xor(block % 2, half) * 32
        + jnp.bitwise_xor(block // 2, core) * 16
        + source % 16
    )
    order = (place == target).astype(BF16)
    return jnp.einsum("lrc,cd->lrd", blocks, order, preferred_element_type=BF16)


def local(
    wave_now, wave_prev, courant, rec_index, rec_history, green, lag_delay, emit_cells, emit_weights
):
    shots = wave_now.shape[0]
    receivers = rec_index.reshape(-1)
    rows_hot = (
        lax.shift_right_logical(receivers, 7)[:, None] == jnp.arange(TILE * TILE)[None, :]
    ).astype(BF16)
    lanes_hot = (
        jnp.bitwise_and(receivers, DEPTH - 1)[:, None] == jnp.arange(DEPTH)[None, :]
    ).astype(F32)
    halos = halo_blocks(wave_now, wave_prev, courant)
    old_all = spread_rows(rec_history.reshape(shots * HIST, -1))
    green, _ = lax.optimization_barrier((green, halos[4:]))
    wide_green = gathered_green(green)
    field, wave_last, new_here = stencil(wave_now, wave_prev, courant, halos, rows_hot, lanes_hot)
    new_all = spread_rows(new_here)
    partial = columns(lag_delay, old_all, new_all, wide_green)
    summed = jnp.sum(lax.all_to_all(partial, ("tx", "ty"), 0, 0, tiled=True), axis=0)
    em = row_exchange(summed.reshape(8, 16, 128))
    wave_out, emission = inject(
        em, emit_cells.reshape(emit_cells.shape[-2:]), emit_weights.reshape(emit_weights.shape[-2:]), field
    )
    return wave_out, wave_last, emission.reshape(shots, STEPS, 1, 1, -1)


def solution(mesh):
    return jax.shard_map(
        local,
        mesh=mesh,
        in_specs=(
            P("shot", "tx", "ty", None),
            P("shot", "tx", "ty", None),
            P("tx", "ty", None),
            P("tx", "ty", None),
            P("shot", None, "tx", "ty", None),
            P(None, ("tx", "ty"), "shot"),
            P(),
            P("tx", "ty", None, None),
            P("tx", "ty", None, None),
        ),
        out_specs=(
            P("shot", "tx", "ty", None),
            P("shot", "tx", "ty", None),
            P("shot", None, "tx", "ty", None),
        ),
        check_vma=False,
    )
```

```python
import jax
import jax.numpy as jnp
from jax import lax
from jax.experimental import pallas as pl
from jax.experimental.pallas import tpu as pltpu
from jax.sharding import PartitionSpec as P


STEPS = 8
HIST = 8
BAND = 8
TILE = 16
WIDE = TILE + 2 * BAND
DEPTH = 128
PAD = 8
F32 = jnp.float32
BF16 = jnp.bfloat16
NT = (((1,), (1,)), ((), ()))


def shot_id(half, row, core):
    return (half * 8 + row) * 2 + core


SHOT_COORDS = [(h, r, c) for h in range(2) for r in range(8) for c in range(2)]
CORE_SWAP = [(shot_id(h, r, c), shot_id(h, r, 1 - c)) for h, r, c in SHOT_COORDS]
HALF_SWAP = [(shot_id(h, r, c), shot_id(1 - h, r, c)) for h, r, c in SHOT_COORDS]
ROW_GROUPS = [[shot_id(h, r, c) for r in range(8)] for h in range(2) for c in range(2)]
UP = [(i, i + 1) for i in range(3)]
DOWN = [(i + 1, i) for i in range(3)]


def row_exchange(x):
    return lax.all_to_all(
        x, "shot", split_axis=0, concat_axis=0, tiled=True, axis_index_groups=ROW_GROUPS
    )


def spread_rows(x):
    return row_exchange(jnp.broadcast_to(x[None], (8, *x.shape)))


def stencil_kernel(
    now, prev, speed_in, xm, xp, ym, yp, cmm, cmp, cpm, cpp, rows_hot, lanes_hot,
    next_out, last_out, rec_out, cur, prv, spd, sems, out_sems,
):
    shots = now.shape[0]
    low = slice(0, BAND)
    mid = slice(BAND, BAND + TILE)
    high = slice(BAND + TILE, WIDE)
    ylow = slice(PAD, PAD + BAND)
    ymid = slice(PAD + BAND, PAD + BAND + TILE)
    yhigh = slice(PAD + BAND + TILE, PAD + WIDE)
    copies = []

    def add(src, dst):
        copies.append(pltpu.make_async_copy(src, dst, sems.at[len(copies)]))

    add(now, cur.at[:, mid, ymid])
    add(prev, prv.at[:, mid, ymid])
    add(speed_in, spd.at[mid, ymid])
    for block, xs, ys in (
        (xm, low, ymid), (xp, high, ymid), (ym, mid, ylow), (yp, mid, yhigh),
        (cmm, low, ylow), (cmp, low, yhigh), (cpm, high, ylow), (cpp, high, yhigh),
    ):
        add(block.at[pl.ds(0, shots)], cur.at[:, xs, ys])
        add(block.at[pl.ds(shots, shots)], prv.at[:, xs, ys])
        add(block.at[2 * shots], spd.at[xs, ys])
    for copy in copies:
        copy.start()
    for copy in copies:
        copy.wait()

    bufs = (cur, prv)
    lanes = lax.broadcasted_iota(jnp.int32, (WIDE, DEPTH), 1)
    sel_row = lax.broadcasted_iota(jnp.int32, (shots * STEPS, shots * DEPTH), 0)
    sel_col = lax.broadcasted_iota(jnp.int32, (shots * STEPS, shots * DEPTH), 1)
    records = jnp.zeros((shots * STEPS, rows_hot.shape[0]), F32)
    for step in range(1, STEPS + 1):
        src, dst = bufs[(step - 1) % 2], bufs[step % 2]
        if step < STEPS:
            start, count = PAD, WIDE
        else:
            start, count = PAD + BAND, TILE
        lane = lanes[:count]

        def body(x, carry, src=src, dst=dst, start=start, count=count, lane=lane):
            speed = spd[x, pl.ds(start, count), :]
            centre = 2.0 - 6.0 * speed
            for s in range(shots):
                u = src[s, x, pl.ds(start, count), :]
                total = src[s, x - 1, pl.ds(start, count), :] + src[s, x + 1, pl.ds(start, count), :]
                total = total + src[s, x, pl.ds(start - 1, count), :]
                total = total + src[s, x, pl.ds(start + 1, count), :]
                total = total + jnp.where(lane > 0, pltpu.roll(u, 1, 1), 0.0)
                total = total + jnp.where(lane < DEPTH - 1, pltpu.roll(u, DEPTH - 1, 1), 0.0)
                dst[s, x, pl.ds(start, count), :] = (
                    centre * u - dst[s, x, pl.ds(start, count), :] + speed * total
                )
            return carry

        lax.fori_loop(step, WIDE - step, body, 0)
        if step < STEPS:
            field = jnp.concatenate(
                [dst[s, mid, ymid, :].reshape(TILE * TILE, DEPTH).astype(BF16) for s in range(shots)],
                axis=1,
            )
            picked = jnp.dot(rows_hot[...], field, preferred_element_type=F32)
            mask = jnp.concatenate([lanes_hot[...]] * shots, axis=1)
            picked = (picked * mask).astype(BF16)
            sel = (sel_row == (sel_col // DEPTH) * STEPS + (step - 1)).astype(F32).astype(BF16)
            records = records + lax.dot_general(sel, picked, NT, preferred_element_type=F32)
    rec_out[...] = records.astype(BF16)
    out_next = pltpu.make_async_copy(bufs[STEPS % 2].at[:, mid, ymid], next_out, out_sems.at[0])
    out_last = pltpu.make_async_copy(bufs[(STEPS - 1) % 2].at[:, mid, ymid], last_out, out_sems.at[1])
    out_next.start()
    out_last.start()
    out_next.wait()
    out_last.wait()


def stencil(now, prev, speed, halos, rows_hot, lanes_hot):
    shots = now.shape[0]
    points = rows_hot.shape[0]
    anywhere = pl.BlockSpec(memory_space=pl.ANY)
    vmem = pl.BlockSpec(memory_space=pltpu.VMEM)
    wide = (shots, WIDE, WIDE + 2 * PAD, DEPTH)
    return pl.pallas_call(
        stencil_kernel,
        out_shape=(
            jax.ShapeDtypeStruct(now.shape, F32),
            jax.ShapeDtypeStruct(now.shape, F32),
            jax.ShapeDtypeStruct((shots * STEPS, points), BF16),
        ),
        in_specs=[anywhere] * 11 + [vmem] * 2,
        out_specs=(anywhere, anywhere, vmem),
        scratch_shapes=[
            pltpu.VMEM(wide, F32),
            pltpu.VMEM(wide, F32),
            pltpu.VMEM(wide[1:], F32),
            pltpu.SemaphoreType.DMA((27,)),
            pltpu.SemaphoreType.DMA((2,)),
        ],
        compiler_params=pltpu.CompilerParams(vmem_limit_bytes=16 << 20),
        cost_estimate=pl.CostEstimate(flops=2_000_000_000, bytes_accessed=12_000_000, transcendentals=0),
        name="stencil",
    )(now, prev, speed, *halos, rows_hot, lanes_hot)


def columns_kernel(delay, old, new, green, out):
    groups, rows, _ = old.shape
    half = rows // 2
    lags = green.shape[0]
    width = green.shape[2]
    sel_row = lax.broadcasted_iota(jnp.int32, (half, 2 * rows), 0)
    sel_col = lax.broadcasted_iota(jnp.int32, (half, 2 * rows), 1)
    col_shot = (sel_col % rows) // STEPS
    col_time = (sel_col // rows) * HIST + sel_col % STEPS
    both = [jnp.concatenate([old[g], new[g]], axis=0) for g in range(groups)]
    parts = []
    for h in range(2):
        row_shot = sel_row // STEPS + h * (half // STEPS)
        total = None
        for lag in range(lags):
            wanted = HIST + sel_row % STEPS - delay[lag]
            sel = jnp.logical_and(col_shot == row_shot, col_time == wanted)
            sel = sel.astype(F32).astype(BF16)
            window = jnp.concatenate(
                [jnp.dot(sel, b, preferred_element_type=F32).astype(BF16) for b in both], axis=0
            )
            term = jnp.dot(window, green[lag], preferred_element_type=F32)
            total = term if total is None else total + term
        parts.append(total)
    lane = lax.broadcasted_iota(jnp.int32, (groups * half, 128), 1)
    for m in range(width // 128):
        a = parts[0][:, m * 128 : (m + 1) * 128]
        b = parts[1][:, m * 128 : (m + 1) * 128]
        out[2 * m] = jnp.where(lane < 64, a, pltpu.roll(b, 64, 1))
        out[2 * m + 1] = jnp.where(lane < 64, pltpu.roll(a, 64, 1), b)


def columns(delay, old, new, green):
    vmem = pl.BlockSpec(memory_space=pltpu.VMEM)
    return pl.pallas_call(
        columns_kernel,
        out_shape=jax.ShapeDtypeStruct((16, 128, 128), F32),
        in_specs=[pl.BlockSpec(memory_space=pltpu.SMEM), vmem, vmem, vmem],
        out_specs=vmem,
        compiler_params=pltpu.CompilerParams(vmem_limit_bytes=12 << 20),
        cost_estimate=pl.CostEstimate(flops=1_000_000_000, bytes_accessed=4_000_000, transcendentals=0),
        name="columns",
    )(delay, old, new, green)


def inject_kernel(em, cells, weights, field, wave_out, emission, rhs_high, rhs_low, acc):
    shots = field.shape[0]
    points = cells.shape[1]
    lane = lax.broadcasted_iota(jnp.int32, (16, 128), 1)
    for sh in range(2):
        for tile in range(4):
            z = tile // 2
            block = None
            for i in range(4):
                piece = em[(tile % 2) * 4 + i]
                shift = (i * 32 - sh * 64 - z * 32) % 128
                if shift:
                    piece = pltpu.roll(piece, shift, 1)
                block = piece if block is None else jnp.where(lane >= i * 32, piece, block)
            emission[pl.ds(sh * 16, 16), pl.ds(tile * 128, 128)] = block

    acc[...] = jnp.zeros_like(acc)
    row_iota = lax.broadcasted_iota(jnp.int32, (TILE * TILE, points), 0)
    lane_iota = lax.broadcasted_iota(jnp.int32, (DEPTH, points), 0)

    def body(k, carry):
        cell = cells[pl.ds(k, 1), :]
        weight = weights[pl.ds(k, 1), :]
        rows_hot = (row_iota == lax.shift_right_logical(cell, 7)).astype(F32).astype(BF16)
        lane_hot = lane_iota == jnp.bitwise_and(cell, DEPTH - 1)
        for s in range(shots):
            value = weight * emission[pl.ds(s * STEPS + STEPS - 1, 1), :]
            top = value.astype(BF16).astype(F32)
            rest = value - top
            rhs_high[pl.ds(s * DEPTH, DEPTH), :] = jnp.where(lane_hot, top, 0.0).astype(BF16)
            rhs_low[pl.ds(s * DEPTH, DEPTH), :] = jnp.where(lane_hot, rest, 0.0).astype(BF16)
        acc[...] += lax.dot_general(
            rows_hot, rhs_high[...], NT, preferred_element_type=F32
        ) + lax.dot_general(rows_hot, rhs_low[...], NT, preferred_element_type=F32)
        return carry

    lax.fori_loop(0, cells.shape[0], body, 0)
    for s in range(shots):
        wave_out[s] = field[s] + acc[:, s * DEPTH : (s + 1) * DEPTH].reshape(TILE, TILE, DEPTH)


def inject(em, cells, weights, field):
    shots = field.shape[0]
    points = cells.shape[1]
    vmem = pl.BlockSpec(memory_space=pltpu.VMEM)
    return pl.pallas_call(
        inject_kernel,
        out_shape=(
            jax.ShapeDtypeStruct(field.shape, F32),
            jax.ShapeDtypeStruct((shots * STEPS, points), F32),
        ),
        in_specs=[vmem] * 4,
        out_specs=(vmem, vmem),
        scratch_shapes=[
            pltpu.VMEM((shots * DEPTH, points), BF16),
            pltpu.VMEM((shots * DEPTH, points), BF16),
            pltpu.VMEM((TILE * TILE, shots * DEPTH), F32),
        ],
        compiler_params=pltpu.CompilerParams(vmem_limit_bytes=12 << 20),
        cost_estimate=pl.CostEstimate(flops=4_000_000_000, bytes_accessed=4_000_000, transcendentals=0),
        name="inject",
    )(em, cells, weights, field)


def halo_blocks(now, prev, speed):
    def stacked(xs, ys):
        return jnp.concatenate([now[:, xs, ys], prev[:, xs, ys], speed[None, xs, ys]], 0)

    whole = slice(None)
    head, tail = slice(0, BAND), slice(TILE - BAND, TILE)
    xm = lax.ppermute(stacked(tail, whole), "tx", UP)
    ym = lax.ppermute(stacked(whole, tail), "ty", UP)
    xp = lax.ppermute(stacked(head, whole), "tx", DOWN)
    yp = lax.ppermute(stacked(whole, head), "ty", DOWN)
    cmm = lax.ppermute(ym[:, tail], "tx", UP)
    cpm = lax.ppermute(xp[:, :, tail], "ty", UP)
    cpp = lax.ppermute(yp[:, head], "tx", DOWN)
    cmp = lax.ppermute(xm[:, :, head], "ty", DOWN)
    return xm, xp, ym, yp, cmm, cmp, cpm, cpp


def gathered_green(green):
    other = lax.ppermute(green, "shot", HALF_SWAP)
    mine = jnp.concatenate([green, other], -1)
    theirs = lax.ppermute(mine, "shot", CORE_SWAP)
    blocks = jnp.concatenate([mine, theirs], -1)
    width = blocks.shape[-1]
    me = lax.axis_index("shot")
    half, core = me // 16, me % 2
    source = lax.broadcasted_iota(jnp.int32, (width, width), 0)
    target = lax.broadcasted_iota(jnp.int32, (width, width), 1)
    block = source // 256
    place = (
        (source % 256 // 16) * 64
        + jnp.bitwise_xor(block % 2, half) * 32
        + jnp.bitwise_xor(block // 2, core) * 16
        + source % 16
    )
    order = (place == target).astype(BF16)
    return jnp.einsum("lrc,cd->lrd", blocks, order, preferred_element_type=BF16)


def block(
    wave_now, wave_prev, courant, rec_index, rec_history, green, lag_delay, emit_cells, emit_weights
):
    shots = wave_now.shape[0]
    receivers = rec_index.reshape(-1)
    rows_hot = (
        lax.shift_right_logical(receivers, 7)[:, None] == jnp.arange(TILE * TILE)[None, :]
    ).astype(BF16)
    lanes_hot = (
        jnp.bitwise_and(receivers, DEPTH - 1)[:, None] == jnp.arange(DEPTH)[None, :]
    ).astype(F32)
    halos = halo_blocks(wave_now, wave_prev, courant)
    old_all = spread_rows(rec_history.reshape(shots * HIST, -1))
    wide_green = gathered_green(green)
    field, wave_last, new_here = stencil(wave_now, wave_prev, courant, halos, rows_hot, lanes_hot)
    new_all = spread_rows(new_here)
    partial = columns(lag_delay, old_all, new_all, wide_green)
    partial = lax.all_to_all(partial.reshape(4, 512, 128), "tx", 0, 0, tiled=True)
    partial = jnp.sum(partial, axis=0).reshape(4, 128, 128)
    summed = jnp.sum(lax.all_to_all(partial, "ty", 0, 0, tiled=True), axis=0)
    em = row_exchange(summed.reshape(8, 16, 128))
    wave_out, emission = inject(
        em, emit_cells.reshape(emit_cells.shape[-2:]), emit_weights.reshape(emit_weights.shape[-2:]), field
    )
    return wave_out, wave_last, emission.reshape(shots, STEPS, 1, 1, -1)


def solution(mesh):
    return jax.shard_map(
        block,
        mesh=mesh,
        in_specs=(
            P("shot", "tx", "ty", None),
            P("shot", "tx", "ty", None),
            P("tx", "ty", None),
            P("tx", "ty", None),
            P("shot", None, "tx", "ty", None),
            P(None, ("tx", "ty"), "shot"),
            P(),
            P("tx", "ty", None, None),
            P("tx", "ty", None, None),
        ),
        out_specs=(
            P("shot", "tx", "ty", None),
            P("shot", "tx", "ty", None),
            P("shot", None, "tx", "ty", None),
        ),
        check_vma=False,
    )
```

```python
import jax
import jax.numpy as jnp
from jax import lax
from jax.experimental import pallas as pl
from jax.experimental.pallas import tpu as pltpu
from jax.sharding import PartitionSpec as P


STEPS = 8
HIST = 8
BAND = 8
TILE = 16
WIDE = TILE + 2 * BAND
DEPTH = 128
PAD = 8
F32 = jnp.float32
BF16 = jnp.bfloat16
NT = (((1,), (1,)), ((), ()))


def shot_id(half, row, core):
    return (half * 8 + row) * 2 + core


SHOT_COORDS = [(h, r, c) for h in range(2) for r in range(8) for c in range(2)]
CORE_SWAP = [(shot_id(h, r, c), shot_id(h, r, 1 - c)) for h, r, c in SHOT_COORDS]
PAIR_SWAP = [(shot_id(h, r, c), shot_id(h, r ^ 1, c)) for h, r, c in SHOT_COORDS]
ROW_GROUPS = [
    [shot_id(h, 2 * k + odd, c) for h in range(2) for k in range(4)]
    for odd in range(2)
    for c in range(2)
]
UP = [(i, i + 1) for i in range(3)]
DOWN = [(i + 1, i) for i in range(3)]


def row_exchange(x):
    return lax.all_to_all(
        x, "shot", split_axis=0, concat_axis=0, tiled=True, axis_index_groups=ROW_GROUPS
    )


def spread_rows(x):
    return row_exchange(jnp.broadcast_to(x[None], (8, *x.shape)))


def stencil_kernel(
    now, prev, speed_in, xm, xp, ym, yp, cmm, cmp, cpm, cpp, rows_hot, lanes_hot,
    next_out, last_out, rec_out, cur, prv, spd, sems, out_sems,
):
    shots = now.shape[0]
    low = slice(0, BAND)
    mid = slice(BAND, BAND + TILE)
    high = slice(BAND + TILE, WIDE)
    ylow = slice(PAD, PAD + BAND)
    ymid = slice(PAD + BAND, PAD + BAND + TILE)
    yhigh = slice(PAD + BAND + TILE, PAD + WIDE)
    copies = []

    def add(src, dst):
        copies.append(pltpu.make_async_copy(src, dst, sems.at[len(copies)]))

    add(now, cur.at[:, mid, ymid])
    add(prev, prv.at[:, mid, ymid])
    add(speed_in, spd.at[mid, ymid])
    for block, xs, ys in (
        (xm, low, ymid), (xp, high, ymid), (ym, mid, ylow), (yp, mid, yhigh),
        (cmm, low, ylow), (cmp, low, yhigh), (cpm, high, ylow), (cpp, high, yhigh),
    ):
        add(block.at[pl.ds(0, shots)], cur.at[:, xs, ys])
        add(block.at[pl.ds(shots, shots)], prv.at[:, xs, ys])
        add(block.at[2 * shots], spd.at[xs, ys])
    for copy in copies:
        copy.start()
    for copy in copies:
        copy.wait()

    bufs = (cur, prv)
    lanes = lax.broadcasted_iota(jnp.int32, (WIDE, DEPTH), 1)
    sel_row = lax.broadcasted_iota(jnp.int32, (shots * STEPS, shots * DEPTH), 0)
    sel_col = lax.broadcasted_iota(jnp.int32, (shots * STEPS, shots * DEPTH), 1)
    records = jnp.zeros((shots * STEPS, rows_hot.shape[0]), F32)
    for step in range(1, STEPS + 1):
        src, dst = bufs[(step - 1) % 2], bufs[step % 2]
        if step < STEPS:
            start, count = (PAD, WIDE) if step < 4 else (PAD + 4, WIDE - 8)
        else:
            start, count = PAD + BAND, TILE
        lane = lanes[:count]

        def body(x, carry, src=src, dst=dst, start=start, count=count, lane=lane):
            speed = spd[x, pl.ds(start, count), :]
            centre = 2.0 - 6.0 * speed
            for s in range(shots):
                u = src[s, x, pl.ds(start, count), :]
                total = src[s, x - 1, pl.ds(start, count), :] + src[s, x + 1, pl.ds(start, count), :]
                total = total + src[s, x, pl.ds(start - 1, count), :]
                total = total + src[s, x, pl.ds(start + 1, count), :]
                total = total + jnp.where(lane > 0, pltpu.roll(u, 1, 1), 0.0)
                total = total + jnp.where(lane < DEPTH - 1, pltpu.roll(u, DEPTH - 1, 1), 0.0)
                dst[s, x, pl.ds(start, count), :] = (
                    centre * u - dst[s, x, pl.ds(start, count), :] + speed * total
                )
            return carry

        lax.fori_loop(step, WIDE - step, body, 0, unroll=4)
        if step < STEPS:
            field = jnp.concatenate(
                [dst[s, mid, ymid, :].reshape(TILE * TILE, DEPTH).astype(BF16) for s in range(shots)],
                axis=1,
            )
            picked = jnp.dot(rows_hot[...], field, preferred_element_type=F32)
            mask = jnp.concatenate([lanes_hot[...]] * shots, axis=1)
            picked = (picked * mask).astype(BF16)
            sel = (sel_row == (sel_col // DEPTH) * STEPS + (step - 1)).astype(F32).astype(BF16)
            records = records + lax.dot_general(sel, picked, NT, preferred_element_type=F32)
    rec_out[...] = records.astype(BF16)
    out_next = pltpu.make_async_copy(bufs[STEPS % 2].at[:, mid, ymid], next_out, out_sems.at[0])
    out_last = pltpu.make_async_copy(bufs[(STEPS - 1) % 2].at[:, mid, ymid], last_out, out_sems.at[1])
    out_next.start()
    out_last.start()
    out_next.wait()
    out_last.wait()


def stencil(now, prev, speed, halos, rows_hot, lanes_hot):
    shots = now.shape[0]
    points = rows_hot.shape[0]
    anywhere = pl.BlockSpec(memory_space=pl.ANY)
    vmem = pl.BlockSpec(memory_space=pltpu.VMEM)
    wide = (shots, WIDE, WIDE + 2 * PAD, DEPTH)
    return pl.pallas_call(
        stencil_kernel,
        out_shape=(
            jax.ShapeDtypeStruct(now.shape, F32),
            jax.ShapeDtypeStruct(now.shape, F32),
            jax.ShapeDtypeStruct((shots * STEPS, points), BF16),
        ),
        in_specs=[anywhere] * 11 + [vmem] * 2,
        out_specs=(anywhere, anywhere, vmem),
        scratch_shapes=[
            pltpu.VMEM(wide, F32),
            pltpu.VMEM(wide, F32),
            pltpu.VMEM(wide[1:], F32),
            pltpu.SemaphoreType.DMA((27,)),
            pltpu.SemaphoreType.DMA((2,)),
        ],
        compiler_params=pltpu.CompilerParams(vmem_limit_bytes=16 << 20),
        cost_estimate=pl.CostEstimate(flops=2_000_000_000, bytes_accessed=12_000_000, transcendentals=0),
        name="stencil",
    )(now, prev, speed, *halos, rows_hot, lanes_hot)


def columns_kernel(delay, old, new, green, out):
    groups, rows, _ = old.shape
    half = rows // 2
    lags = green.shape[0]
    width = green.shape[2]
    sel_row = lax.broadcasted_iota(jnp.int32, (half, 2 * rows), 0)
    sel_col = lax.broadcasted_iota(jnp.int32, (half, 2 * rows), 1)
    col_shot = (sel_col % rows) // STEPS
    col_time = (sel_col // rows) * HIST + sel_col % STEPS
    both = [jnp.concatenate([old[g], new[g]], axis=0) for g in range(groups)]
    parts = []
    for h in range(2):
        row_shot = sel_row // STEPS + h * (half // STEPS)
        total = None
        for lag in range(lags):
            wanted = HIST + sel_row % STEPS - delay[lag]
            sel = jnp.logical_and(col_shot == row_shot, col_time == wanted)
            sel = sel.astype(F32).astype(BF16)
            window = jnp.concatenate(
                [jnp.dot(sel, b, preferred_element_type=F32).astype(BF16) for b in both], axis=0
            )
            term = jnp.dot(window, green[lag], preferred_element_type=F32)
            total = term if total is None else total + term
        parts.append(total)
    lane = lax.broadcasted_iota(jnp.int32, (groups * half, 128), 1)
    for m in range(width // 128):
        a = parts[0][:, m * 128 : (m + 1) * 128]
        b = parts[1][:, m * 128 : (m + 1) * 128]
        out[2 * m] = jnp.where(lane < 64, a, pltpu.roll(b, 64, 1))
        out[2 * m + 1] = jnp.where(lane < 64, pltpu.roll(a, 64, 1), b)


def columns(delay, old, new, green):
    vmem = pl.BlockSpec(memory_space=pltpu.VMEM)
    return pl.pallas_call(
        columns_kernel,
        out_shape=jax.ShapeDtypeStruct((16, 128, 128), F32),
        in_specs=[pl.BlockSpec(memory_space=pltpu.SMEM), vmem, vmem, vmem],
        out_specs=vmem,
        compiler_params=pltpu.CompilerParams(vmem_limit_bytes=12 << 20),
        cost_estimate=pl.CostEstimate(flops=1_000_000_000, bytes_accessed=4_000_000, transcendentals=0),
        name="columns",
    )(delay, old, new, green)


def inject_kernel(em, cells, weights, field, wave_out, emission, rhs_high, rhs_low, acc):
    shots = field.shape[0]
    points = cells.shape[1]
    lane = lax.broadcasted_iota(jnp.int32, (16, 128), 1)
    for tile in range(4):
        even, odd = em[2 * tile], em[2 * tile + 1]
        emission[pl.ds(0, 16), pl.ds(tile * 128, 128)] = jnp.where(lane < 64, even, pltpu.roll(odd, 64, 1))
        emission[pl.ds(16, 16), pl.ds(tile * 128, 128)] = jnp.where(lane < 64, pltpu.roll(even, 64, 1), odd)

    acc[...] = jnp.zeros_like(acc)
    row_iota = lax.broadcasted_iota(jnp.int32, (TILE * TILE, points), 0)
    lane_iota = lax.broadcasted_iota(jnp.int32, (DEPTH, points), 0)

    def body(k, carry):
        cell = cells[pl.ds(k, 1), :]
        weight = weights[pl.ds(k, 1), :]
        rows_hot = (row_iota == lax.shift_right_logical(cell, 7)).astype(F32).astype(BF16)
        lane_hot = lane_iota == jnp.bitwise_and(cell, DEPTH - 1)
        for s in range(shots):
            value = weight * emission[pl.ds(s * STEPS + STEPS - 1, 1), :]
            top = value.astype(BF16).astype(F32)
            rest = value - top
            rhs_high[pl.ds(s * DEPTH, DEPTH), :] = jnp.where(lane_hot, top, 0.0).astype(BF16)
            rhs_low[pl.ds(s * DEPTH, DEPTH), :] = jnp.where(lane_hot, rest, 0.0).astype(BF16)
        acc[...] += lax.dot_general(
            rows_hot, rhs_high[...], NT, preferred_element_type=F32
        ) + lax.dot_general(rows_hot, rhs_low[...], NT, preferred_element_type=F32)
        return carry

    lax.fori_loop(0, cells.shape[0], body, 0)
    for s in range(shots):
        wave_out[s] = field[s] + acc[:, s * DEPTH : (s + 1) * DEPTH].reshape(TILE, TILE, DEPTH)


def inject(em, cells, weights, field):
    shots = field.shape[0]
    points = cells.shape[1]
    vmem = pl.BlockSpec(memory_space=pltpu.VMEM)
    return pl.pallas_call(
        inject_kernel,
        out_shape=(
            jax.ShapeDtypeStruct(field.shape, F32),
            jax.ShapeDtypeStruct((shots * STEPS, points), F32),
        ),
        in_specs=[vmem] * 4,
        out_specs=(vmem, vmem),
        scratch_shapes=[
            pltpu.VMEM((shots * DEPTH, points), BF16),
            pltpu.VMEM((shots * DEPTH, points), BF16),
            pltpu.VMEM((TILE * TILE, shots * DEPTH), F32),
        ],
        compiler_params=pltpu.CompilerParams(vmem_limit_bytes=12 << 20),
        cost_estimate=pl.CostEstimate(flops=4_000_000_000, bytes_accessed=4_000_000, transcendentals=0),
        name="inject",
    )(em, cells, weights, field)


def pack_kernel(now, prev, speed, xtail, ytail, xhead, yhead):
    shots = now.shape[0]
    head, tail = slice(0, BAND), slice(TILE - BAND, TILE)
    for out, xs, ys in (
        (xtail, tail, slice(None)), (ytail, slice(None), tail),
        (xhead, head, slice(None)), (yhead, slice(None), head),
    ):
        out[pl.ds(0, shots)] = now[:, xs, ys]
        out[pl.ds(shots, shots)] = prev[:, xs, ys]
        out[2 * shots] = speed[xs, ys]


def packed(now, prev, speed):
    fields = 2 * now.shape[0] + 1
    vmem = pl.BlockSpec(memory_space=pltpu.VMEM)
    across = jax.ShapeDtypeStruct((fields, BAND, TILE, DEPTH), F32)
    along = jax.ShapeDtypeStruct((fields, TILE, BAND, DEPTH), F32)
    return pl.pallas_call(
        pack_kernel,
        out_shape=(across, along, across, along),
        in_specs=[vmem] * 3,
        out_specs=(vmem,) * 4,
        compiler_params=pltpu.CompilerParams(vmem_limit_bytes=8 << 20),
        cost_estimate=pl.CostEstimate(flops=0, bytes_accessed=4_000_000, transcendentals=0),
        name="pack",
    )(now, prev, speed)


def halo_blocks(now, prev, speed):
    xtail, ytail, xhead, yhead = packed(now, prev, speed)
    head, tail = slice(0, BAND), slice(TILE - BAND, TILE)
    xm = lax.ppermute(xtail, "tx", UP)
    ym = lax.ppermute(ytail, "ty", UP)
    xp = lax.ppermute(xhead, "tx", DOWN)
    yp = lax.ppermute(yhead, "ty", DOWN)
    cmm = lax.ppermute(ym[:, tail], "tx", UP)
    cpm = lax.ppermute(xp[:, :, tail], "ty", UP)
    cpp = lax.ppermute(yp[:, head], "tx", DOWN)
    cmp = lax.ppermute(xm[:, :, head], "ty", DOWN)
    return xm, xp, ym, yp, cmm, cmp, cpm, cpp


def gathered_green(green):
    other = lax.ppermute(green, "shot", PAIR_SWAP)
    mine = jnp.concatenate([green, other], -1)
    theirs = lax.ppermute(mine, "shot", CORE_SWAP)
    blocks = jnp.concatenate([mine, theirs], -1)
    width = blocks.shape[-1]
    me = lax.axis_index("shot")
    odd, core = me // 2 % 2, me % 2
    source = lax.broadcasted_iota(jnp.int32, (width, width), 0)
    target = lax.broadcasted_iota(jnp.int32, (width, width), 1)
    block = source // 256
    place = (
        (source % 256 // 16) * 64
        + jnp.bitwise_xor(block % 2, odd) * 32
        + jnp.bitwise_xor(block // 2, core) * 16
        + source % 16
    )
    order = (place == target).astype(BF16)
    return jnp.einsum("lrc,cd->lrd", blocks, order, preferred_element_type=BF16)


def block(
    wave_now, wave_prev, courant, rec_index, rec_history, green, lag_delay, emit_cells, emit_weights
):
    shots = wave_now.shape[0]
    receivers = rec_index.reshape(-1)
    rows_hot = (
        lax.shift_right_logical(receivers, 7)[:, None] == jnp.arange(TILE * TILE)[None, :]
    ).astype(BF16)
    lanes_hot = (
        jnp.bitwise_and(receivers, DEPTH - 1)[:, None] == jnp.arange(DEPTH)[None, :]
    ).astype(F32)
    halos = halo_blocks(wave_now, wave_prev, courant)
    old_all = spread_rows(rec_history.reshape(shots * HIST, -1))
    wide_green = gathered_green(green)
    field, wave_last, new_here = stencil(wave_now, wave_prev, courant, halos, rows_hot, lanes_hot)
    new_all = spread_rows(new_here)
    partial = columns(lag_delay, old_all, new_all, wide_green)
    partial = lax.all_to_all(partial.reshape(4, 512, 128), "tx", 0, 0, tiled=True)
    partial = jnp.sum(partial, axis=0).reshape(4, 128, 128)
    summed = jnp.sum(lax.all_to_all(partial, "ty", 0, 0, tiled=True), axis=0)
    em = row_exchange(summed.reshape(8, 16, 128))
    wave_out, emission = inject(
        em, emit_cells.reshape(emit_cells.shape[-2:]), emit_weights.reshape(emit_weights.shape[-2:]), field
    )
    return wave_out, wave_last, emission.reshape(shots, STEPS, 1, 1, -1)


def solution(mesh):
    return jax.shard_map(
        block,
        mesh=mesh,
        in_specs=(
            P("shot", "tx", "ty", None),
            P("shot", "tx", "ty", None),
            P("tx", "ty", None),
            P("tx", "ty", None),
            P("shot", None, "tx", "ty", None),
            P(None, ("tx", "ty"), "shot"),
            P(),
            P("tx", "ty", None, None),
            P("tx", "ty", None, None),
        ),
        out_specs=(
            P("shot", "tx", "ty", None),
            P("shot", "tx", "ty", None),
            P("shot", None, "tx", "ty", None),
        ),
        check_vma=False,
    )
```

```python
import jax
import jax.numpy as jnp
from jax import lax
from jax.experimental import pallas as pl
from jax.experimental.pallas import tpu as pltpu
from jax.sharding import PartitionSpec as P


STEPS = 8
HIST = 8
BAND = 8
TILE = 16
WIDE = TILE + 2 * BAND
DEPTH = 128
PAD = 8
F32 = jnp.float32
BF16 = jnp.bfloat16
NT = (((1,), (1,)), ((), ()))


def shot_id(half, row, core):
    return (half * 8 + row) * 2 + core


SHOT_COORDS = [(h, r, c) for h in range(2) for r in range(8) for c in range(2)]
CORE_SWAP = [(shot_id(h, r, c), shot_id(h, r, 1 - c)) for h, r, c in SHOT_COORDS]
DIAG_SWAP = [(shot_id(h, r, c), shot_id(h, r ^ 1, 1 - c)) for h, r, c in SHOT_COORDS]
PAIR_SWAP = [(shot_id(h, r, c), shot_id(h, r ^ 1, c)) for h, r, c in SHOT_COORDS]
ROW_GROUPS = [
    [shot_id(h, 2 * k + odd, c) for h in range(2) for k in range(4)]
    for odd in range(2)
    for c in range(2)
]
UP = [(i, i + 1) for i in range(3)]
DOWN = [(i + 1, i) for i in range(3)]


def in_hbm(*arrays):
    return tuple(pltpu.with_memory_space_constraint(x, pltpu.HBM) for x in arrays)


def row_exchange(x):
    return lax.all_to_all(
        x, "shot", split_axis=0, concat_axis=0, tiled=True, axis_index_groups=ROW_GROUPS
    )


def spread_rows(x):
    return row_exchange(jnp.broadcast_to(x[None], (8, *x.shape)))


def stencil_kernel(
    now, prev, speed_in, xm, xp, ym, yp, cmm, cmp, cpm, cpp, rows_hot, lanes_hot, history,
    next_out, last_out, rec_out, cur, prv, spd, sems, out_sems,
):
    shots = now.shape[0]
    low = slice(0, BAND)
    mid = slice(BAND, BAND + TILE)
    high = slice(BAND + TILE, WIDE)
    ylow = slice(PAD, PAD + BAND)
    ymid = slice(PAD + BAND, PAD + BAND + TILE)
    yhigh = slice(PAD + BAND + TILE, PAD + WIDE)
    copies = []

    def add(src, dst):
        copies.append(pltpu.make_async_copy(src, dst, sems.at[len(copies)]))

    add(now, cur.at[:, mid, ymid])
    add(prev, prv.at[:, mid, ymid])
    add(speed_in, spd.at[mid, ymid])
    for block, xs, ys in (
        (xm, low, ymid), (xp, high, ymid), (ym, mid, ylow), (yp, mid, yhigh),
        (cmm, low, ylow), (cmp, low, yhigh), (cpm, high, ylow), (cpp, high, yhigh),
    ):
        add(block.at[pl.ds(0, shots)], cur.at[:, xs, ys])
        add(block.at[pl.ds(shots, shots)], prv.at[:, xs, ys])
        add(block.at[2 * shots], spd.at[xs, ys])
    for copy in copies:
        copy.start()
    for copy in copies:
        copy.wait()

    bufs = (cur, prv)
    lanes = lax.broadcasted_iota(jnp.int32, (WIDE, DEPTH), 1)
    sel_row = lax.broadcasted_iota(jnp.int32, (shots * STEPS, shots * DEPTH), 0)
    sel_col = lax.broadcasted_iota(jnp.int32, (shots * STEPS, shots * DEPTH), 1)
    records = jnp.zeros((shots * STEPS, rows_hot.shape[0]), F32)
    for step in range(1, STEPS + 1):
        src, dst = bufs[(step - 1) % 2], bufs[step % 2]
        if step < STEPS:
            start, count = (PAD, WIDE) if step < 4 else (PAD + 4, WIDE - 8)
        else:
            start, count = PAD + BAND, TILE
        lane = lanes[:count]

        def body(x, carry, src=src, dst=dst, start=start, count=count, lane=lane):
            speed = spd[x, pl.ds(start, count), :]
            centre = 2.0 - 6.0 * speed
            for s in range(shots):
                u = src[s, x, pl.ds(start, count), :]
                total = src[s, x - 1, pl.ds(start, count), :] + src[s, x + 1, pl.ds(start, count), :]
                total = total + src[s, x, pl.ds(start - 1, count), :]
                total = total + src[s, x, pl.ds(start + 1, count), :]
                total = total + jnp.where(lane > 0, pltpu.roll(u, 1, 1), 0.0)
                total = total + jnp.where(lane < DEPTH - 1, pltpu.roll(u, DEPTH - 1, 1), 0.0)
                dst[s, x, pl.ds(start, count), :] = (
                    centre * u - dst[s, x, pl.ds(start, count), :] + speed * total
                )
            return carry

        lax.fori_loop(step, WIDE - step, body, 0, unroll=4)
        if step < STEPS:
            field = jnp.concatenate(
                [dst[s, mid, ymid, :].reshape(TILE * TILE, DEPTH).astype(BF16) for s in range(shots)],
                axis=1,
            )
            picked = jnp.dot(rows_hot[...], field, preferred_element_type=F32)
            mask = jnp.concatenate([lanes_hot[...]] * shots, axis=1)
            picked = (picked * mask).astype(BF16)
            sel = (sel_row == (sel_col // DEPTH) * STEPS + (step - 1)).astype(F32).astype(BF16)
            records = records + lax.dot_general(sel, picked, NT, preferred_element_type=F32)
    rec_out[pl.ds(0, shots * HIST), :] = history[...]
    rec_out[pl.ds(shots * HIST, shots * STEPS), :] = records.astype(BF16)
    out_next = pltpu.make_async_copy(bufs[STEPS % 2].at[:, mid, ymid], next_out, out_sems.at[0])
    out_last = pltpu.make_async_copy(bufs[(STEPS - 1) % 2].at[:, mid, ymid], last_out, out_sems.at[1])
    out_next.start()
    out_last.start()
    out_next.wait()
    out_last.wait()


def stencil(now, prev, speed, halos, rows_hot, lanes_hot, history):
    shots = now.shape[0]
    points = rows_hot.shape[0]
    anywhere = pl.BlockSpec(memory_space=pl.ANY)
    vmem = pl.BlockSpec(memory_space=pltpu.VMEM)
    hbm = pl.BlockSpec(memory_space=pltpu.HBM)
    wide = (shots, WIDE, WIDE + 2 * PAD, DEPTH)
    return pl.pallas_call(
        stencil_kernel,
        out_shape=(
            jax.ShapeDtypeStruct(now.shape, F32),
            jax.ShapeDtypeStruct(now.shape, F32),
            jax.ShapeDtypeStruct((shots * (HIST + STEPS), points), BF16),
        ),
        in_specs=[hbm] * 3 + [anywhere] * 8 + [vmem] * 3,
        out_specs=(hbm, hbm, vmem),
        scratch_shapes=[
            pltpu.VMEM(wide, F32),
            pltpu.VMEM(wide, F32),
            pltpu.VMEM(wide[1:], F32),
            pltpu.SemaphoreType.DMA((27,)),
            pltpu.SemaphoreType.DMA((2,)),
        ],
        compiler_params=pltpu.CompilerParams(vmem_limit_bytes=16 << 20),
        cost_estimate=pl.CostEstimate(flops=2_000_000_000, bytes_accessed=12_000_000, transcendentals=0),
        name="stencil",
    )(*in_hbm(now, prev, speed), *halos, rows_hot, lanes_hot, history)


def columns_kernel(delay, records, green, out):
    groups, rows, _ = records.shape
    rows = rows // 2
    half = rows // 2
    lags = green.shape[0]
    width = green.shape[2]
    sel_row = lax.broadcasted_iota(jnp.int32, (half, 2 * rows), 0)
    sel_col = lax.broadcasted_iota(jnp.int32, (half, 2 * rows), 1)
    col_shot = (sel_col % rows) // STEPS
    col_time = (sel_col // rows) * HIST + sel_col % STEPS
    both = [records[g] for g in range(groups)]
    parts = []
    for h in range(2):
        row_shot = sel_row // STEPS + h * (half // STEPS)
        total = None
        for lag in range(lags):
            wanted = HIST + sel_row % STEPS - delay[lag]
            sel = jnp.logical_and(col_shot == row_shot, col_time == wanted)
            sel = sel.astype(F32).astype(BF16)
            window = jnp.concatenate(
                [jnp.dot(sel, b, preferred_element_type=F32).astype(BF16) for b in both], axis=0
            )
            term = jnp.dot(window, green[lag], preferred_element_type=F32)
            total = term if total is None else total + term
        parts.append(total)
    lane = lax.broadcasted_iota(jnp.int32, (groups * half, 128), 1)
    for m in range(width // 128):
        a = parts[0][:, m * 128 : (m + 1) * 128]
        b = parts[1][:, m * 128 : (m + 1) * 128]
        out[2 * m] = jnp.where(lane < 64, a, pltpu.roll(b, 64, 1))
        out[2 * m + 1] = jnp.where(lane < 64, pltpu.roll(a, 64, 1), b)


def columns(delay, records, green):
    vmem = pl.BlockSpec(memory_space=pltpu.VMEM)
    return pl.pallas_call(
        columns_kernel,
        out_shape=jax.ShapeDtypeStruct((16, 128, 128), F32),
        in_specs=[pl.BlockSpec(memory_space=pltpu.SMEM), vmem, vmem],
        out_specs=vmem,
        compiler_params=pltpu.CompilerParams(vmem_limit_bytes=12 << 20),
        cost_estimate=pl.CostEstimate(flops=1_000_000_000, bytes_accessed=4_000_000, transcendentals=0),
        name="columns",
    )(delay, records, green)


def inject_kernel(em, cells, weights, field, wave_out, emission_out, rhs_high, rhs_low, acc, emission):
    shots = field.shape[0]
    points = cells.shape[1]
    lane = lax.broadcasted_iota(jnp.int32, (16, 128), 1)
    for tile in range(4):
        even, odd = em[2 * tile], em[2 * tile + 1]
        emission[pl.ds(0, 16), pl.ds(tile * 128, 128)] = jnp.where(lane < 64, even, pltpu.roll(odd, 64, 1))
        emission[pl.ds(16, 16), pl.ds(tile * 128, 128)] = jnp.where(lane < 64, pltpu.roll(even, 64, 1), odd)

    acc[...] = jnp.zeros_like(acc)
    row_iota = lax.broadcasted_iota(jnp.int32, (TILE * TILE, points), 0)
    lane_iota = lax.broadcasted_iota(jnp.int32, (DEPTH, points), 0)

    def body(k, carry):
        cell = cells[pl.ds(k, 1), :]
        weight = weights[pl.ds(k, 1), :]
        rows_hot = (row_iota == lax.shift_right_logical(cell, 7)).astype(F32).astype(BF16)
        lane_hot = lane_iota == jnp.bitwise_and(cell, DEPTH - 1)
        for s in range(shots):
            value = weight * emission[pl.ds(s * STEPS + STEPS - 1, 1), :]
            top = value.astype(BF16).astype(F32)
            rest = value - top
            rhs_high[pl.ds(s * DEPTH, DEPTH), :] = jnp.where(lane_hot, top, 0.0).astype(BF16)
            rhs_low[pl.ds(s * DEPTH, DEPTH), :] = jnp.where(lane_hot, rest, 0.0).astype(BF16)
        acc[...] += lax.dot_general(
            rows_hot, rhs_high[...], NT, preferred_element_type=F32
        ) + lax.dot_general(rows_hot, rhs_low[...], NT, preferred_element_type=F32)
        return carry

    lax.fori_loop(0, cells.shape[0], body, 0)
    for row in range(shots * STEPS):
        emission_out[row] = emission[pl.ds(row, 1), :]
    for s in range(shots):
        wave_out[s] = field[s] + acc[:, s * DEPTH : (s + 1) * DEPTH].reshape(TILE, TILE, DEPTH)


def inject(em, cells, weights, field):
    shots = field.shape[0]
    points = cells.shape[1]
    vmem = pl.BlockSpec(memory_space=pltpu.VMEM)
    return pl.pallas_call(
        inject_kernel,
        out_shape=(
            jax.ShapeDtypeStruct(field.shape, F32),
            jax.ShapeDtypeStruct((shots * STEPS, 1, points), F32),
        ),
        in_specs=[vmem] * 4,
        out_specs=(vmem, vmem),
        scratch_shapes=[
            pltpu.VMEM((shots * DEPTH, points), BF16),
            pltpu.VMEM((shots * DEPTH, points), BF16),
            pltpu.VMEM((TILE * TILE, shots * DEPTH), F32),
            pltpu.VMEM((shots * STEPS, points), F32),
        ],
        compiler_params=pltpu.CompilerParams(vmem_limit_bytes=12 << 20),
        cost_estimate=pl.CostEstimate(flops=4_000_000_000, bytes_accessed=4_000_000, transcendentals=0),
        name="inject",
    )(em, cells, weights, field)


def pack_kernel(now, prev, speed, xtail, ytail, xhead, yhead, field, sems):
    shots = now.shape[0]
    copies = [
        pltpu.make_async_copy(now, field.at[pl.ds(0, shots)], sems.at[0]),
        pltpu.make_async_copy(prev, field.at[pl.ds(shots, shots)], sems.at[1]),
        pltpu.make_async_copy(speed, field.at[2 * shots], sems.at[2]),
    ]
    for copy in copies:
        copy.start()
    for copy in copies:
        copy.wait()
    head, tail = slice(0, BAND), slice(TILE - BAND, TILE)
    xtail[...] = field[:, tail]
    ytail[...] = field[:, :, tail]
    xhead[...] = field[:, head]
    yhead[...] = field[:, :, head]


def packed(now, prev, speed):
    fields = 2 * now.shape[0] + 1
    vmem = pl.BlockSpec(memory_space=pltpu.VMEM)
    across = jax.ShapeDtypeStruct((fields, BAND, TILE, DEPTH), F32)
    along = jax.ShapeDtypeStruct((fields, TILE, BAND, DEPTH), F32)
    return pl.pallas_call(
        pack_kernel,
        out_shape=(across, along, across, along),
        in_specs=[pl.BlockSpec(memory_space=pltpu.HBM)] * 3,
        out_specs=(vmem,) * 4,
        scratch_shapes=[
            pltpu.VMEM((fields, TILE, TILE, DEPTH), F32),
            pltpu.SemaphoreType.DMA((3,)),
        ],
        compiler_params=pltpu.CompilerParams(vmem_limit_bytes=8 << 20),
        cost_estimate=pl.CostEstimate(flops=0, bytes_accessed=4_000_000, transcendentals=0),
        name="pack",
    )(*in_hbm(now, prev, speed))


def halo_blocks(now, prev, speed):
    xtail, ytail, xhead, yhead = packed(now, prev, speed)
    head, tail = slice(0, BAND), slice(TILE - BAND, TILE)
    xm = lax.ppermute(xtail, "tx", UP)
    ym = lax.ppermute(ytail, "ty", UP)
    xp = lax.ppermute(xhead, "tx", DOWN)
    yp = lax.ppermute(yhead, "ty", DOWN)
    cmm = lax.ppermute(ym[:, tail], "tx", UP)
    cpm = lax.ppermute(xp[:, :, tail], "ty", UP)
    cpp = lax.ppermute(yp[:, head], "tx", DOWN)
    cmp = lax.ppermute(xm[:, :, head], "ty", DOWN)
    return xm, xp, ym, yp, cmm, cmp, cpm, cpp


def order_kernel(place, own_in, pair_in, core_in, diag_in, out, own, pair, core, diag, sems):
    copies = [
        pltpu.make_async_copy(src, dst, sems.at[i])
        for i, (src, dst) in enumerate(
            ((own_in, own), (pair_in, pair), (core_in, core), (diag_in, diag))
        )
    ]
    for copy in copies:
        copy.start()
    for copy in copies:
        copy.wait()
    lags, _, width = own.shape
    source = lax.broadcasted_iota(jnp.int32, (256, 512), 0)
    target = lax.broadcasted_iota(jnp.int32, (256, 512), 1)
    local = source % 128
    other_row = source // 128
    for lag in range(lags):
        for m in range(width // 128):
            cut = pl.ds(m * 128, 128)
            total = None
            for other_core, (a, b) in enumerate(((own, pair), (core, diag))):
                spot = (
                    (local // 16) * 64
                    + jnp.bitwise_xor(other_row, place[0]) * 32
                    + jnp.bitwise_xor(other_core, place[1]) * 16
                    + local % 16
                )
                hot = (spot == target).astype(F32).astype(BF16)
                both = jnp.concatenate([a[lag, :, cut], b[lag, :, cut]], axis=1)
                term = jnp.dot(both, hot, preferred_element_type=F32)
                total = term if total is None else total + term
            out[lag, :, pl.ds(m * 512, 512)] = total.astype(BF16)


def gathered_green(green):
    def moved(pairs):
        return lax.ppermute(green, "shot", pairs)

    core = moved(CORE_SWAP)
    pair = moved(PAIR_SWAP)
    diag = moved(DIAG_SWAP)
    me = lax.axis_index("shot")
    place = jnp.stack([me // 2 % 2, me % 2]).astype(jnp.int32)
    lags, points, width = green.shape
    vmem = pl.BlockSpec(memory_space=pltpu.VMEM)
    return pl.pallas_call(
        order_kernel,
        out_shape=jax.ShapeDtypeStruct((lags, points, 4 * width), BF16),
        in_specs=[pl.BlockSpec(memory_space=pltpu.SMEM)]
        + [pl.BlockSpec(memory_space=pltpu.HBM)] * 4,
        out_specs=vmem,
        scratch_shapes=[pltpu.VMEM(green.shape, BF16)] * 4 + [pltpu.SemaphoreType.DMA((4,))],
        compiler_params=pltpu.CompilerParams(vmem_limit_bytes=12 << 20),
        cost_estimate=pl.CostEstimate(flops=1_000_000_000, bytes_accessed=4_000_000, transcendentals=0),
        name="order",
    )(place, *in_hbm(green, pair, core, diag))


def block(
    wave_now, wave_prev, courant, rec_index, rec_history, green, lag_delay, emit_cells, emit_weights
):
    shots = wave_now.shape[0]
    receivers = rec_index.reshape(-1)
    rows_hot = (
        lax.shift_right_logical(receivers, 7)[:, None] == jnp.arange(TILE * TILE)[None, :]
    ).astype(BF16)
    lanes_hot = (
        jnp.bitwise_and(receivers, DEPTH - 1)[:, None] == jnp.arange(DEPTH)[None, :]
    ).astype(F32)
    halos = halo_blocks(wave_now, wave_prev, courant)
    wide_green = gathered_green(green)
    field, wave_last, records = stencil(
        wave_now, wave_prev, courant, halos, rows_hot, lanes_hot, rec_history.reshape(shots * HIST, -1)
    )
    records = spread_rows(records)
    partial = columns(lag_delay, records, wide_green)
    partial = lax.all_to_all(partial.reshape(4, 512, 128), "tx", 0, 0, tiled=True)
    partial = jnp.sum(partial, axis=0).reshape(4, 128, 128)
    summed = jnp.sum(lax.all_to_all(partial, "ty", 0, 0, tiled=True), axis=0)
    em = row_exchange(summed.reshape(8, 16, 128))
    wave_out, emission = inject(
        em, emit_cells.reshape(emit_cells.shape[-2:]), emit_weights.reshape(emit_weights.shape[-2:]), field
    )
    return wave_out, wave_last, emission.reshape(shots, STEPS, 1, 1, -1)


def solution(mesh):
    return jax.shard_map(
        block,
        mesh=mesh,
        in_specs=(
            P("shot", "tx", "ty", None),
            P("shot", "tx", "ty", None),
            P("tx", "ty", None),
            P("tx", "ty", None),
            P("shot", None, "tx", "ty", None),
            P(None, ("tx", "ty"), "shot"),
            P(),
            P("tx", "ty", None, None),
            P("tx", "ty", None, None),
        ),
        out_specs=(
            P("shot", "tx", "ty", None),
            P("shot", "tx", "ty", None),
            P("shot", None, "tx", "ty", None),
        ),
        check_vma=False,
    )
```

```python
import jax
import jax.numpy as jnp
from jax import lax
from jax.experimental import pallas as pl
from jax.experimental.pallas import tpu as pltpu
from jax.sharding import PartitionSpec as P


STEPS = 8
HIST = 8
BAND = 8
TILE = 16
WIDE = TILE + 2 * BAND
DEPTH = 128
PAD = 8
F32 = jnp.float32
BF16 = jnp.bfloat16
NT = (((1,), (1,)), ((), ()))


def shot_id(half, row, core):
    return (half * 8 + row) * 2 + core


SHOT_COORDS = [(h, r, c) for h in range(2) for r in range(8) for c in range(2)]
CORE_SWAP = [(shot_id(h, r, c), shot_id(h, r, 1 - c)) for h, r, c in SHOT_COORDS]
PAIR_SWAP = [(shot_id(h, r, c), shot_id(h, r ^ 1, c)) for h, r, c in SHOT_COORDS]
ROW_GROUPS = [
    [shot_id(h, 2 * k + odd, c) for h in range(2) for k in range(4)]
    for odd in range(2)
    for c in range(2)
]
COLUMN_GROUPS = [
    [shot_id(h, 2 * k + odd, c) for k in range(4)]
    for h in range(2)
    for odd in range(2)
    for c in range(2)
]
RING_GROUPS = [
    [shot_id(h, r, c) * 4 + b for h in range(2) for b in range(4)] for r in range(8) for c in range(2)
]
UP = [(i, i + 1) for i in range(3)]
DOWN = [(i + 1, i) for i in range(3)]


def in_hbm(*arrays):
    return tuple(pltpu.with_memory_space_constraint(x, pltpu.HBM) for x in arrays)


def row_exchange(x):
    return lax.all_to_all(
        x, "shot", split_axis=0, concat_axis=0, tiled=True, axis_index_groups=ROW_GROUPS
    )


def stencil_kernel(
    now, prev, speed_in, xm, xp, ym, yp, cmm, cmp, cpm, cpp, rows_hot, lanes_hot, history,
    next_out, last_out, rec_out, cur, prv, spd, sems, out_sems,
):
    shots = now.shape[0]
    low = slice(0, BAND)
    mid = slice(BAND, BAND + TILE)
    high = slice(BAND + TILE, WIDE)
    ylow = slice(PAD, PAD + BAND)
    ymid = slice(PAD + BAND, PAD + BAND + TILE)
    yhigh = slice(PAD + BAND + TILE, PAD + WIDE)
    copies = []

    def add(src, dst):
        copies.append(pltpu.make_async_copy(src, dst, sems.at[len(copies)]))

    add(now, cur.at[:, mid, ymid])
    add(prev, prv.at[:, mid, ymid])
    add(speed_in, spd.at[mid, ymid])
    for block, xs, ys in (
        (xm, low, ymid), (xp, high, ymid), (ym, mid, ylow), (yp, mid, yhigh),
        (cmm, low, ylow), (cmp, low, yhigh), (cpm, high, ylow), (cpp, high, yhigh),
    ):
        add(block.at[pl.ds(0, shots)], cur.at[:, xs, ys])
        add(block.at[pl.ds(shots, shots)], prv.at[:, xs, ys])
        add(block.at[2 * shots], spd.at[xs, ys])
    for copy in copies:
        copy.start()
    for copy in copies:
        copy.wait()

    bufs = (cur, prv)
    lanes = lax.broadcasted_iota(jnp.int32, (WIDE, DEPTH), 1)
    sel_row = lax.broadcasted_iota(jnp.int32, (shots * STEPS, shots * DEPTH), 0)
    sel_col = lax.broadcasted_iota(jnp.int32, (shots * STEPS, shots * DEPTH), 1)
    records = jnp.zeros((shots * STEPS, rows_hot.shape[0]), F32)
    for step in range(1, STEPS + 1):
        src, dst = bufs[(step - 1) % 2], bufs[step % 2]
        if step < STEPS:
            start, count = (PAD, WIDE) if step < 4 else (PAD + 4, WIDE - 8)
        else:
            start, count = PAD + BAND, TILE
        lane = lanes[:count]

        def body(x, carry, src=src, dst=dst, start=start, count=count, lane=lane):
            speed = spd[x, pl.ds(start, count), :]
            centre = 2.0 - 6.0 * speed
            for s in range(shots):
                u = src[s, x, pl.ds(start, count), :]
                total = src[s, x - 1, pl.ds(start, count), :] + src[s, x + 1, pl.ds(start, count), :]
                total = total + src[s, x, pl.ds(start - 1, count), :]
                total = total + src[s, x, pl.ds(start + 1, count), :]
                total = total + jnp.where(lane > 0, pltpu.roll(u, 1, 1), 0.0)
                total = total + jnp.where(lane < DEPTH - 1, pltpu.roll(u, DEPTH - 1, 1), 0.0)
                dst[s, x, pl.ds(start, count), :] = (
                    centre * u - dst[s, x, pl.ds(start, count), :] + speed * total
                )
            return carry

        lax.fori_loop(step, WIDE - step, body, 0, unroll=4)
        if step < STEPS:
            field = jnp.concatenate(
                [dst[s, mid, ymid, :].reshape(TILE * TILE, DEPTH).astype(BF16) for s in range(shots)],
                axis=1,
            )
            picked = jnp.dot(rows_hot[...], field, preferred_element_type=F32)
            mask = jnp.concatenate([lanes_hot[...]] * shots, axis=1)
            picked = (picked * mask).astype(BF16)
            sel = (sel_row == (sel_col // DEPTH) * STEPS + (step - 1)).astype(F32).astype(BF16)
            records = records + lax.dot_general(sel, picked, NT, preferred_element_type=F32)
    records = records.astype(BF16)
    for group in range(rec_out.shape[0]):
        rec_out[group, pl.ds(0, shots * HIST), :] = history[...]
        rec_out[group, pl.ds(shots * HIST, shots * STEPS), :] = records
    out_next = pltpu.make_async_copy(bufs[STEPS % 2].at[:, mid, ymid], next_out, out_sems.at[0])
    out_last = pltpu.make_async_copy(bufs[(STEPS - 1) % 2].at[:, mid, ymid], last_out, out_sems.at[1])
    out_next.start()
    out_last.start()
    out_next.wait()
    out_last.wait()


def stencil(now, prev, speed, halos, rows_hot, lanes_hot, history):
    shots = now.shape[0]
    points = rows_hot.shape[0]
    anywhere = pl.BlockSpec(memory_space=pl.ANY)
    vmem = pl.BlockSpec(memory_space=pltpu.VMEM)
    hbm = pl.BlockSpec(memory_space=pltpu.HBM)
    wide = (shots, WIDE, WIDE + 2 * PAD, DEPTH)
    return pl.pallas_call(
        stencil_kernel,
        out_shape=(
            jax.ShapeDtypeStruct(now.shape, F32),
            jax.ShapeDtypeStruct(now.shape, F32),
            jax.ShapeDtypeStruct((8, shots * (HIST + STEPS), points), BF16),
        ),
        in_specs=[hbm] * 3 + [anywhere] * 8 + [vmem] * 3,
        out_specs=(hbm, hbm, vmem),
        scratch_shapes=[
            pltpu.VMEM(wide, F32),
            pltpu.VMEM(wide, F32),
            pltpu.VMEM(wide[1:], F32),
            pltpu.SemaphoreType.DMA((27,)),
            pltpu.SemaphoreType.DMA((2,)),
        ],
        compiler_params=pltpu.CompilerParams(vmem_limit_bytes=16 << 20),
        cost_estimate=pl.CostEstimate(flops=2_000_000_000, bytes_accessed=12_000_000, transcendentals=0),
        name="stencil",
    )(*in_hbm(now, prev, speed), *halos, rows_hot, lanes_hot, history)


def columns_kernel(delay, records, green, out):
    groups, rows, _ = records.shape
    rows = rows // 2
    half = rows // 2
    lags = green.shape[0]
    width = green.shape[2]
    sel_row = lax.broadcasted_iota(jnp.int32, (half, 2 * rows), 0)
    sel_col = lax.broadcasted_iota(jnp.int32, (half, 2 * rows), 1)
    col_shot = (sel_col % rows) // STEPS
    col_time = (sel_col // rows) * HIST + sel_col % STEPS
    both = [records[g] for g in range(groups)]
    parts = []
    for h in range(2):
        row_shot = sel_row // STEPS + h * (half // STEPS)
        total = None
        for lag in range(lags):
            wanted = HIST + sel_row % STEPS - delay[lag]
            sel = jnp.logical_and(col_shot == row_shot, col_time == wanted)
            sel = sel.astype(F32).astype(BF16)
            window = jnp.concatenate(
                [jnp.dot(sel, b, preferred_element_type=F32).astype(BF16) for b in both], axis=0
            )
            term = jnp.dot(window, green[lag], preferred_element_type=F32)
            total = term if total is None else total + term
        parts.append(total)
    lane = lax.broadcasted_iota(jnp.int32, (groups * half, 128), 1)
    for m in range(width // 128):
        a = parts[0][:, m * 128 : (m + 1) * 128]
        b = parts[1][:, m * 128 : (m + 1) * 128]
        out[2 * m] = jnp.where(lane < 64, a, pltpu.roll(b, 64, 1))
        out[2 * m + 1] = jnp.where(lane < 64, pltpu.roll(a, 64, 1), b)


def columns(delay, records, green):
    vmem = pl.BlockSpec(memory_space=pltpu.VMEM)
    return pl.pallas_call(
        columns_kernel,
        out_shape=jax.ShapeDtypeStruct((16, 128, 128), F32),
        in_specs=[pl.BlockSpec(memory_space=pltpu.SMEM), vmem, vmem],
        out_specs=vmem,
        compiler_params=pltpu.CompilerParams(vmem_limit_bytes=12 << 20),
        cost_estimate=pl.CostEstimate(flops=1_000_000_000, bytes_accessed=4_000_000, transcendentals=0),
        name="columns",
    )(delay, records, green)


def inject_kernel(em, cells, weights, field, wave_out, emission_out, rhs_high, rhs_low, acc, emission):
    shots = field.shape[0]
    points = cells.shape[1]
    lane = lax.broadcasted_iota(jnp.int32, (16, 128), 1)
    for tile in range(4):
        even, odd = em[2 * tile % 4, tile // 2], em[2 * tile % 4 + 1, tile // 2]
        emission[pl.ds(0, 16), pl.ds(tile * 128, 128)] = jnp.where(lane < 64, even, pltpu.roll(odd, 64, 1))
        emission[pl.ds(16, 16), pl.ds(tile * 128, 128)] = jnp.where(lane < 64, pltpu.roll(even, 64, 1), odd)

    acc[...] = jnp.zeros_like(acc)
    row_iota = lax.broadcasted_iota(jnp.int32, (TILE * TILE, points), 0)
    lane_iota = lax.broadcasted_iota(jnp.int32, (DEPTH, points), 0)

    def body(k, carry):
        cell = cells[pl.ds(k, 1), :]
        weight = weights[pl.ds(k, 1), :]
        rows_hot = (row_iota == lax.shift_right_logical(cell, 7)).astype(F32).astype(BF16)
        lane_hot = lane_iota == jnp.bitwise_and(cell, DEPTH - 1)
        for s in range(shots):
            value = weight * emission[pl.ds(s * STEPS + STEPS - 1, 1), :]
            top = value.astype(BF16).astype(F32)
            rest = value - top
            rhs_high[pl.ds(s * DEPTH, DEPTH), :] = jnp.where(lane_hot, top, 0.0).astype(BF16)
            rhs_low[pl.ds(s * DEPTH, DEPTH), :] = jnp.where(lane_hot, rest, 0.0).astype(BF16)
        acc[...] += lax.dot_general(
            rows_hot, rhs_high[...], NT, preferred_element_type=F32
        ) + lax.dot_general(rows_hot, rhs_low[...], NT, preferred_element_type=F32)
        return carry

    lax.fori_loop(0, cells.shape[0], body, 0)
    for row in range(shots * STEPS):
        emission_out[row] = emission[pl.ds(row, 1), :]
    for s in range(shots):
        wave_out[s] = field[s] + acc[:, s * DEPTH : (s + 1) * DEPTH].reshape(TILE, TILE, DEPTH)


def inject(em, cells, weights, field):
    shots = field.shape[0]
    points = cells.shape[1]
    vmem = pl.BlockSpec(memory_space=pltpu.VMEM)
    return pl.pallas_call(
        inject_kernel,
        out_shape=(
            jax.ShapeDtypeStruct(field.shape, F32),
            jax.ShapeDtypeStruct((shots * STEPS, 1, points), F32),
        ),
        in_specs=[vmem] * 4,
        out_specs=(vmem, vmem),
        scratch_shapes=[
            pltpu.VMEM((shots * DEPTH, points), BF16),
            pltpu.VMEM((shots * DEPTH, points), BF16),
            pltpu.VMEM((TILE * TILE, shots * DEPTH), F32),
            pltpu.VMEM((shots * STEPS, points), F32),
        ],
        compiler_params=pltpu.CompilerParams(vmem_limit_bytes=12 << 20),
        cost_estimate=pl.CostEstimate(flops=4_000_000_000, bytes_accessed=4_000_000, transcendentals=0),
        name="inject",
    )(em, cells, weights, field)


def pack_kernel(now, prev, speed, xtail, ytail, xhead, yhead, field, sems):
    shots = now.shape[0]
    copies = [
        pltpu.make_async_copy(now, field.at[pl.ds(0, shots)], sems.at[0]),
        pltpu.make_async_copy(prev, field.at[pl.ds(shots, shots)], sems.at[1]),
        pltpu.make_async_copy(speed, field.at[2 * shots], sems.at[2]),
    ]
    for copy in copies:
        copy.start()
    for copy in copies:
        copy.wait()
    head, tail = slice(0, BAND), slice(TILE - BAND, TILE)
    xtail[...] = field[:, tail]
    ytail[...] = field[:, :, tail]
    xhead[...] = field[:, head]
    yhead[...] = field[:, :, head]


def packed(now, prev, speed):
    fields = 2 * now.shape[0] + 1
    vmem = pl.BlockSpec(memory_space=pltpu.VMEM)
    across = jax.ShapeDtypeStruct((fields, BAND, TILE, DEPTH), F32)
    along = jax.ShapeDtypeStruct((fields, TILE, BAND, DEPTH), F32)
    return pl.pallas_call(
        pack_kernel,
        out_shape=(across, along, across, along),
        in_specs=[pl.BlockSpec(memory_space=pltpu.HBM)] * 3,
        out_specs=(vmem,) * 4,
        scratch_shapes=[
            pltpu.VMEM((fields, TILE, TILE, DEPTH), F32),
            pltpu.SemaphoreType.DMA((3,)),
        ],
        compiler_params=pltpu.CompilerParams(vmem_limit_bytes=8 << 20),
        cost_estimate=pl.CostEstimate(flops=0, bytes_accessed=4_000_000, transcendentals=0),
        name="pack",
    )(*in_hbm(now, prev, speed))


def halo_blocks(now, prev, speed):
    xtail, ytail, xhead, yhead = packed(now, prev, speed)
    head, tail = slice(0, BAND), slice(TILE - BAND, TILE)
    xm = lax.ppermute(xtail, "tx", UP)
    ym = lax.ppermute(ytail, "ty", UP)
    xp = lax.ppermute(xhead, "tx", DOWN)
    yp = lax.ppermute(yhead, "ty", DOWN)
    cmm = lax.ppermute(ym[:, tail], "tx", UP)
    cpm = lax.ppermute(xp[:, :, tail], "ty", UP)
    cpp = lax.ppermute(yp[:, head], "tx", DOWN)
    cmp = lax.ppermute(xm[:, :, head], "ty", DOWN)
    return xm, xp, ym, yp, cmm, cmp, cpm, cpp


def order_kernel(place, own_in, pair_in, core_in, diag_in, out, own, pair, core, diag, sems):
    copies = [
        pltpu.make_async_copy(src, dst, sems.at[i])
        for i, (src, dst) in enumerate(
            ((own_in, own), (pair_in, pair), (core_in, core), (diag_in, diag))
        )
    ]
    for copy in copies:
        copy.start()
    for copy in copies:
        copy.wait()
    lags, _, width = own.shape
    source = lax.broadcasted_iota(jnp.int32, (256, 512), 0)
    target = lax.broadcasted_iota(jnp.int32, (256, 512), 1)
    local = source % 128
    other_row = source // 128
    for lag in range(lags):
        for m in range(width // 128):
            cut = pl.ds(m * 128, 128)
            total = None
            for other_core, (a, b) in enumerate(((own, pair), (core, diag))):
                spot = (
                    (local // 16) * 64
                    + jnp.bitwise_xor(other_row, place[0]) * 32
                    + jnp.bitwise_xor(other_core, place[1]) * 16
                    + local % 16
                )
                hot = (spot == target).astype(F32).astype(BF16)
                both = jnp.concatenate([a[lag, :, cut], b[lag, :, cut]], axis=1)
                term = jnp.dot(both, hot, preferred_element_type=F32)
                total = term if total is None else total + term
            out[lag, :, pl.ds(m * 512, 512)] = total.astype(BF16)


def gathered_green(green):
    def moved(block, pairs):
        return lax.ppermute(block, "shot", pairs)

    pair = moved(green, PAIR_SWAP)
    core = moved(green, CORE_SWAP)
    diag = moved(pair, CORE_SWAP)
    me = lax.axis_index("shot")
    place = jnp.stack([me // 2 % 2, me % 2]).astype(jnp.int32)
    lags, points, width = green.shape
    vmem = pl.BlockSpec(memory_space=pltpu.VMEM)
    return pl.pallas_call(
        order_kernel,
        out_shape=jax.ShapeDtypeStruct((lags, points, 4 * width), BF16),
        in_specs=[pl.BlockSpec(memory_space=pltpu.SMEM)]
        + [pl.BlockSpec(memory_space=pltpu.HBM)] * 4,
        out_specs=vmem,
        scratch_shapes=[pltpu.VMEM(green.shape, BF16)] * 4 + [pltpu.SemaphoreType.DMA((4,))],
        compiler_params=pltpu.CompilerParams(vmem_limit_bytes=12 << 20),
        cost_estimate=pl.CostEstimate(flops=1_000_000_000, bytes_accessed=4_000_000, transcendentals=0),
        name="order",
    )(place, *in_hbm(green, pair, core, diag))


def block(
    wave_now, wave_prev, courant, rec_index, rec_history, green, lag_delay, emit_cells, emit_weights
):
    shots = wave_now.shape[0]
    receivers = rec_index.reshape(-1)
    rows_hot = (
        lax.shift_right_logical(receivers, 7)[:, None] == jnp.arange(TILE * TILE)[None, :]
    ).astype(BF16)
    lanes_hot = (
        jnp.bitwise_and(receivers, DEPTH - 1)[:, None] == jnp.arange(DEPTH)[None, :]
    ).astype(F32)
    halos = halo_blocks(wave_now, wave_prev, courant)
    wide_green = gathered_green(green)
    field, wave_last, records = stencil(
        wave_now, wave_prev, courant, halos, rows_hot, lanes_hot, rec_history.reshape(shots * HIST, -1)
    )
    records = row_exchange(records)
    partial = columns(lag_delay, records, wide_green)
    partial = lax.all_to_all(partial.reshape(4, 512, 128), "tx", 0, 0, tiled=True)
    partial = jnp.sum(partial, axis=0).reshape(4, 2, 64, 128)
    partial = jnp.swapaxes(partial, 0, 1).reshape(8, 64, 128)
    partial = lax.all_to_all(
        partial, ("shot", "ty"), 0, 0, tiled=True, axis_index_groups=RING_GROUPS
    )
    summed = jnp.sum(partial.reshape(2, 4, 64, 128), axis=1)
    summed = jnp.swapaxes(summed.reshape(2, 4, 16, 128), 0, 1)
    em = lax.all_to_all(
        summed, "shot", 0, 0, tiled=True, axis_index_groups=COLUMN_GROUPS
    )
    wave_out, emission = inject(
        em, emit_cells.reshape(emit_cells.shape[-2:]), emit_weights.reshape(emit_weights.shape[-2:]), field
    )
    return wave_out, wave_last, emission.reshape(shots, STEPS, 1, 1, -1)


def solution(mesh):
    return jax.shard_map(
        block,
        mesh=mesh,
        in_specs=(
            P("shot", "tx", "ty", None),
            P("shot", "tx", "ty", None),
            P("tx", "ty", None),
            P("tx", "ty", None),
            P("shot", None, "tx", "ty", None),
            P(None, ("tx", "ty"), "shot"),
            P(),
            P("tx", "ty", None, None),
            P("tx", "ty", None, None),
        ),
        out_specs=(
            P("shot", "tx", "ty", None),
            P("shot", "tx", "ty", None),
            P("shot", None, "tx", "ty", None),
        ),
        check_vma=False,
    )
```

```python
import jax
import jax.numpy as jnp
from jax import lax
from jax.experimental import pallas as pl
from jax.experimental.pallas import tpu as pltpu
from jax.sharding import PartitionSpec as P


STEPS = 8
HIST = 8
BAND = 8
TILE = 16
WIDE = TILE + 2 * BAND
DEPTH = 128
PAD = 8
F32 = jnp.float32
BF16 = jnp.bfloat16
NT = (((1,), (1,)), ((), ()))


def shot_id(half, row, core):
    return (half * 8 + row) * 2 + core


SHOT_COORDS = [(h, r, c) for h in range(2) for r in range(8) for c in range(2)]
CORE_SWAP = [(shot_id(h, r, c), shot_id(h, r, 1 - c)) for h, r, c in SHOT_COORDS]
PAIR_SWAP = [(shot_id(h, r, c), shot_id(h, r ^ 1, c)) for h, r, c in SHOT_COORDS]
ROW_GROUPS = [
    [shot_id(h, 2 * k + odd, c) for h in range(2) for k in range(4)]
    for odd in range(2)
    for c in range(2)
]
COLUMN_GROUPS = [
    [shot_id(h, 2 * k + odd, c) for k in range(4)]
    for h in range(2)
    for odd in range(2)
    for c in range(2)
]
RING_GROUPS = [
    [shot_id(h, r, c) * 4 + b for h in range(2) for b in range(4)] for r in range(8) for c in range(2)
]
UP = [(i, i + 1) for i in range(3)]
DOWN = [(i + 1, i) for i in range(3)]


def in_hbm(*arrays):
    return tuple(pltpu.with_memory_space_constraint(x, pltpu.HBM) for x in arrays)


def row_exchange(x):
    return lax.all_to_all(
        x, "shot", split_axis=0, concat_axis=0, tiled=True, axis_index_groups=ROW_GROUPS
    )


LOW = slice(0, BAND)
MID = slice(BAND, BAND + TILE)
HIGH = slice(BAND + TILE, WIDE)
YLOW = slice(PAD, PAD + BAND)
YMID = slice(PAD + BAND, PAD + BAND + TILE)
YHIGH = slice(PAD + BAND + TILE, PAD + WIDE)
NEAR = slice(BAND - 1, BAND + TILE + 1)
YNEAR = slice(PAD, PAD + WIDE)
HBM = pl.BlockSpec(memory_space=pltpu.HBM)
ANY = pl.BlockSpec(memory_space=pl.ANY)
VMEM = pl.BlockSpec(memory_space=pltpu.VMEM)


def band_copies(blocks, cur, prv, spd, sems):
    shots = cur.shape[0]
    copies = []
    for block, xs, ys in blocks:
        for src, dst in (
            (block.at[pl.ds(0, shots)], cur.at[:, xs, ys]),
            (block.at[pl.ds(shots, shots)], prv.at[:, xs, ys]),
            (block.at[2 * shots], spd.at[xs, ys]),
        ):
            copies.append(pltpu.make_async_copy(src, dst, sems.at[len(copies)]))
    return copies


def run(copies):
    for copy in copies:
        copy.start()
    for copy in copies:
        copy.wait()


def assemble_kernel(now, prev, speed, xm, xp, ym, yp, cur, prv, spd, own_sems, sems):
    own = [
        pltpu.make_async_copy(now, cur.at[:, MID, YMID], own_sems.at[0]),
        pltpu.make_async_copy(prev, prv.at[:, MID, YMID], own_sems.at[1]),
        pltpu.make_async_copy(speed, spd.at[MID, YMID], own_sems.at[2]),
    ]
    blocks = ((xm, LOW, YMID), (xp, HIGH, YMID), (ym, MID, YLOW), (yp, MID, YHIGH))
    run(own + band_copies(blocks, cur, prv, spd, sems))


def assemble(now, prev, speed, halos):
    shots = now.shape[0]
    wide = (shots, WIDE, WIDE + 2 * PAD, DEPTH)
    return pl.pallas_call(
        assemble_kernel,
        out_shape=(
            jax.ShapeDtypeStruct(wide, F32),
            jax.ShapeDtypeStruct(wide, F32),
            jax.ShapeDtypeStruct(wide[1:], F32),
        ),
        in_specs=[HBM] * 3 + [ANY] * 4,
        out_specs=(VMEM,) * 3,
        scratch_shapes=[pltpu.SemaphoreType.DMA((3,)), pltpu.SemaphoreType.DMA((12,))],
        compiler_params=pltpu.CompilerParams(vmem_limit_bytes=10 << 20),
        cost_estimate=pl.CostEstimate(flops=0, bytes_accessed=8_000_000, transcendentals=0),
        name="assemble",
    )(*in_hbm(now, prev, speed), *halos)


def advance(src, dst, spd, rows, start, count, shift=0, base=0):
    lane = lax.broadcasted_iota(jnp.int32, (count, DEPTH), 1)

    def body(x, carry):
        at, cells = x - shift, pl.ds(start - base, count)
        speed = spd[at, cells, :]
        centre = 2.0 - 6.0 * speed
        for s in range(src.shape[0]):
            u = src[s, x, pl.ds(start, count), :]
            total = src[s, x - 1, pl.ds(start, count), :] + src[s, x + 1, pl.ds(start, count), :]
            total = total + src[s, x, pl.ds(start - 1, count), :]
            total = total + src[s, x, pl.ds(start + 1, count), :]
            total = total + jnp.where(lane > 0, pltpu.roll(u, 1, 1), 0.0)
            total = total + jnp.where(lane < DEPTH - 1, pltpu.roll(u, DEPTH - 1, 1), 0.0)
            dst[s, at, cells, :] = centre * u - dst[s, at, cells, :] + speed * total
        return carry

    lax.fori_loop(*rows, body, 0, unroll=4)


def stencil_kernel(
    cur_in, prv_in, spd_in, cmm, cmp, cpm, cpp, rows_hot, lanes_hot, history,
    rec_out, near_out, before_out, cur, prv, spd, rec, sems, out_sems,
):
    shots = cur.shape[0]
    blocks = ((cmm, LOW, YLOW), (cmp, LOW, YHIGH), (cpm, HIGH, YLOW), (cpp, HIGH, YHIGH))
    run(band_copies(blocks, cur, prv, spd, sems))
    bufs = (cur, prv)
    sel_row = lax.broadcasted_iota(jnp.int32, (shots * STEPS, shots * DEPTH), 0)
    sel_col = lax.broadcasted_iota(jnp.int32, (shots * STEPS, shots * DEPTH), 1)
    mask = jnp.concatenate([lanes_hot[...]] * shots, axis=1)
    records = jnp.zeros((shots * STEPS, rows_hot.shape[0]), F32)
    for step in range(1, STEPS):
        src, dst = bufs[(step - 1) % 2], bufs[step % 2]
        start, count = (PAD, WIDE) if step < 4 else (PAD + 4, WIDE - 8)
        advance(src, dst, spd, (step, WIDE - step), start, count)
        field = jnp.concatenate(
            [dst[s, MID, YMID, :].reshape(TILE * TILE, DEPTH).astype(BF16) for s in range(shots)],
            axis=1,
        )
        picked = jnp.dot(rows_hot[...], field, preferred_element_type=F32)
        picked = (picked * mask).astype(BF16)
        sel = (sel_row == (sel_col // DEPTH) * STEPS + (step - 1)).astype(F32).astype(BF16)
        records = records + lax.dot_general(sel, picked, NT, preferred_element_type=F32)
    rec[pl.ds(0, shots * HIST), :] = history[...]
    rec[pl.ds(shots * HIST, shots * STEPS), :] = records.astype(BF16)
    run(
        [pltpu.make_async_copy(rec, rec_out.at[g], out_sems.at[g]) for g in range(8)]
        + [
            pltpu.make_async_copy(prv.at[:, NEAR, YNEAR], near_out, out_sems.at[8]),
            pltpu.make_async_copy(cur.at[:, MID, YMID], before_out, out_sems.at[9]),
        ]
    )


def stencil(cur, prv, spd, corners, rows_hot, lanes_hot, history):
    shots = cur.shape[0]
    points = rows_hot.shape[0]
    return pl.pallas_call(
        stencil_kernel,
        out_shape=(
            jax.ShapeDtypeStruct((8, shots * (HIST + STEPS), points), BF16),
            jax.ShapeDtypeStruct((shots, TILE + 2, WIDE, DEPTH), F32),
            jax.ShapeDtypeStruct((shots, TILE, TILE, DEPTH), F32),
            jax.ShapeDtypeStruct(cur.shape, F32),
            jax.ShapeDtypeStruct(cur.shape, F32),
            jax.ShapeDtypeStruct(spd.shape, F32),
        ),
        in_specs=[VMEM] * 3 + [ANY] * 4 + [VMEM] * 3,
        out_specs=(HBM,) * 3 + (VMEM,) * 3,
        input_output_aliases={0: 3, 1: 4, 2: 5},
        scratch_shapes=[
            pltpu.VMEM((shots * (HIST + STEPS), points), BF16),
            pltpu.SemaphoreType.DMA((12,)),
            pltpu.SemaphoreType.DMA((10,)),
        ],
        compiler_params=pltpu.CompilerParams(vmem_limit_bytes=20 << 20),
        cost_estimate=pl.CostEstimate(flops=2_000_000_000, bytes_accessed=12_000_000, transcendentals=0),
        name="stencil",
    )(cur, prv, spd, *corners, rows_hot, lanes_hot, history)


def late_kernel(near, before, spd, cells, last, field, rows_hot, lanes_hot):
    middle = slice(BAND, BAND + TILE)
    last[...] = near[:, 1 : TILE + 1, middle, :]
    field[...] = before[...]
    advance(near, field, spd, (1, TILE + 1), BAND, TILE, shift=1, base=BAND)
    points = cells.shape[1]
    row_iota = lax.broadcasted_iota(jnp.int32, (TILE * TILE, points), 0)
    lane_iota = lax.broadcasted_iota(jnp.int32, (DEPTH, points), 0)

    def body(k, carry):
        cell = cells[pl.ds(k, 1), :]
        rows_hot[k] = (row_iota == lax.shift_right_logical(cell, 7)).astype(F32).astype(BF16)
        lanes_hot[k] = (lane_iota == jnp.bitwise_and(cell, DEPTH - 1)).astype(F32).astype(BF16)
        return carry

    lax.fori_loop(0, cells.shape[0], body, 0)


def late(near, before, speed, cells):
    corners, points = cells.shape
    return pl.pallas_call(
        late_kernel,
        out_shape=(
            jax.ShapeDtypeStruct(before.shape, F32),
            jax.ShapeDtypeStruct(before.shape, F32),
            jax.ShapeDtypeStruct((corners, TILE * TILE, points), BF16),
            jax.ShapeDtypeStruct((corners, DEPTH, points), BF16),
        ),
        in_specs=[VMEM] * 4,
        out_specs=(VMEM,) * 4,
        compiler_params=pltpu.CompilerParams(vmem_limit_bytes=20 << 20),
        cost_estimate=pl.CostEstimate(flops=200_000_000, bytes_accessed=12_000_000, transcendentals=0),
        name="late",
    )(near, before, speed, cells)


def columns_kernel(delay, records, green, pieces, out, sems):
    groups, rows, _ = records.shape
    rows = rows // 2
    half = rows // 2
    lags = green.shape[0]
    width = green.shape[2]
    sel_row = lax.broadcasted_iota(jnp.int32, (half, 2 * rows), 0)
    sel_col = lax.broadcasted_iota(jnp.int32, (half, 2 * rows), 1)
    col_shot = (sel_col % rows) // STEPS
    col_time = (sel_col // rows) * HIST + sel_col % STEPS
    both = [records[g] for g in range(groups)]
    parts = []
    for h in range(2):
        row_shot = sel_row // STEPS + h * (half // STEPS)
        total = None
        for lag in range(lags):
            wanted = HIST + sel_row % STEPS - delay[lag]
            sel = jnp.logical_and(col_shot == row_shot, col_time == wanted)
            sel = sel.astype(F32).astype(BF16)
            window = jnp.concatenate(
                [jnp.dot(sel, b, preferred_element_type=F32).astype(BF16) for b in both], axis=0
            )
            term = jnp.dot(window, green[lag], preferred_element_type=F32)
            total = term if total is None else total + term
        parts.append(total)
    lane = lax.broadcasted_iota(jnp.int32, (groups * half, 128), 1)
    copies = []
    for m in range(width // 128):
        a = parts[0][:, m * 128 : (m + 1) * 128]
        b = parts[1][:, m * 128 : (m + 1) * 128]
        out[2 * m] = jnp.where(lane < 64, a, pltpu.roll(b, 64, 1))
        out[2 * m + 1] = jnp.where(lane < 64, pltpu.roll(a, 64, 1), b)
        pair = pl.ds(2 * m, 2)
        copies.append(pltpu.make_async_copy(out.at[pair], pieces.at[pair], sems.at[m]))
        copies[-1].start()
    for copy in copies:
        copy.wait()


def columns(delay, records, green):
    vmem = pl.BlockSpec(memory_space=pltpu.VMEM)
    return pl.pallas_call(
        columns_kernel,
        out_shape=jax.ShapeDtypeStruct((16, 128, 128), F32),
        in_specs=[pl.BlockSpec(memory_space=pltpu.SMEM), vmem, vmem],
        out_specs=pl.BlockSpec(memory_space=pltpu.HBM),
        scratch_shapes=[pltpu.VMEM((16, 128, 128), F32), pltpu.SemaphoreType.DMA((8,))],
        compiler_params=pltpu.CompilerParams(vmem_limit_bytes=12 << 20),
        cost_estimate=pl.CostEstimate(flops=1_000_000_000, bytes_accessed=4_000_000, transcendentals=0),
        name="columns",
    )(delay, records, green)


def inject_kernel(
    em, rows_in, lanes_in, weights, field,
    wave_out, emission_out, rhs_high, rhs_low, acc, emission, rows_hot, lanes_hot, sems,
):
    count = weights.shape[0]
    copies = []
    for k in range(count):
        copies.append(pltpu.make_async_copy(rows_in.at[k], rows_hot.at[k], sems.at[k]))
        copies.append(pltpu.make_async_copy(lanes_in.at[k], lanes_hot.at[k], sems.at[count + k]))
    for copy in copies:
        copy.start()
    shots = field.shape[0]
    lane = lax.broadcasted_iota(jnp.int32, (16, 128), 1)
    for tile in range(4):
        even, odd = em[2 * tile % 4, tile // 2], em[2 * tile % 4 + 1, tile // 2]
        emission[pl.ds(0, 16), pl.ds(tile * 128, 128)] = jnp.where(lane < 64, even, pltpu.roll(odd, 64, 1))
        emission[pl.ds(16, 16), pl.ds(tile * 128, 128)] = jnp.where(lane < 64, pltpu.roll(even, 64, 1), odd)

    acc[...] = jnp.zeros_like(acc)

    def body(k, carry):
        pltpu.make_async_copy(rows_in.at[k], rows_hot.at[k], sems.at[k]).wait()
        pltpu.make_async_copy(lanes_in.at[k], lanes_hot.at[k], sems.at[count + k]).wait()
        weight = weights[pl.ds(k, 1), :]
        hot = lanes_hot[k]
        for s in range(shots):
            value = weight * emission[pl.ds(s * STEPS + STEPS - 1, 1), :]
            top = value.astype(BF16)
            rest = (value - top.astype(F32)).astype(BF16)
            rhs_high[pl.ds(s * DEPTH, DEPTH), :] = hot * top
            rhs_low[pl.ds(s * DEPTH, DEPTH), :] = hot * rest
        acc[...] += lax.dot_general(
            rows_hot[k], rhs_high[...], NT, preferred_element_type=F32
        ) + lax.dot_general(rows_hot[k], rhs_low[...], NT, preferred_element_type=F32)
        return carry

    lax.fori_loop(0, weights.shape[0], body, 0)
    for row in range(shots * STEPS):
        emission_out[row] = emission[pl.ds(row, 1), :]
    for s in range(shots):
        wave_out[s] = field[s] + acc[:, s * DEPTH : (s + 1) * DEPTH].reshape(TILE, TILE, DEPTH)


def inject(em, rows_hot, lanes_hot, weights, field):
    shots = field.shape[0]
    points = weights.shape[1]
    vmem = pl.BlockSpec(memory_space=pltpu.VMEM)
    return pl.pallas_call(
        inject_kernel,
        out_shape=(
            jax.ShapeDtypeStruct((shots, TILE, TILE, DEPTH), F32),
            jax.ShapeDtypeStruct((shots * STEPS, 1, points), F32),
        ),
        in_specs=[vmem] + [pl.BlockSpec(memory_space=pltpu.HBM)] * 2 + [vmem] * 2,
        out_specs=(vmem, vmem),
        scratch_shapes=[
            pltpu.VMEM((shots * DEPTH, points), BF16),
            pltpu.VMEM((shots * DEPTH, points), BF16),
            pltpu.VMEM((TILE * TILE, shots * DEPTH), F32),
            pltpu.VMEM((shots * STEPS, points), F32),
            pltpu.VMEM(rows_hot.shape, BF16),
            pltpu.VMEM(lanes_hot.shape, BF16),
            pltpu.SemaphoreType.DMA((2 * weights.shape[0],)),
        ],
        compiler_params=pltpu.CompilerParams(vmem_limit_bytes=12 << 20),
        cost_estimate=pl.CostEstimate(flops=4_000_000_000, bytes_accessed=4_000_000, transcendentals=0),
        name="inject",
    )(em, *in_hbm(rows_hot, lanes_hot), weights, field)


def pack_kernel(now, prev, speed, xtail, ytail, xhead, yhead, field, sems):
    shots = now.shape[0]
    copies = [
        pltpu.make_async_copy(now, field.at[pl.ds(0, shots)], sems.at[0]),
        pltpu.make_async_copy(prev, field.at[pl.ds(shots, shots)], sems.at[1]),
        pltpu.make_async_copy(speed, field.at[2 * shots], sems.at[2]),
    ]
    for copy in copies:
        copy.start()
    for copy in copies:
        copy.wait()
    head, tail = slice(0, BAND), slice(TILE - BAND, TILE)
    xtail[...] = field[:, tail]
    ytail[...] = field[:, :, tail]
    xhead[...] = field[:, head]
    yhead[...] = field[:, :, head]


def packed(now, prev, speed):
    fields = 2 * now.shape[0] + 1
    vmem = pl.BlockSpec(memory_space=pltpu.VMEM)
    across = jax.ShapeDtypeStruct((fields, BAND, TILE, DEPTH), F32)
    along = jax.ShapeDtypeStruct((fields, TILE, BAND, DEPTH), F32)
    return pl.pallas_call(
        pack_kernel,
        out_shape=(across, along, across, along),
        in_specs=[pl.BlockSpec(memory_space=pltpu.HBM)] * 3,
        out_specs=(vmem,) * 4,
        scratch_shapes=[
            pltpu.VMEM((fields, TILE, TILE, DEPTH), F32),
            pltpu.SemaphoreType.DMA((3,)),
        ],
        compiler_params=pltpu.CompilerParams(vmem_limit_bytes=8 << 20),
        cost_estimate=pl.CostEstimate(flops=0, bytes_accessed=4_000_000, transcendentals=0),
        name="pack",
    )(*in_hbm(now, prev, speed))


def halo_blocks(now, prev, speed):
    xtail, ytail, xhead, yhead = packed(now, prev, speed)
    head, tail = slice(0, BAND), slice(TILE - BAND, TILE)
    xm = lax.ppermute(xtail, "tx", UP)
    ym = lax.ppermute(ytail, "ty", UP)
    xp = lax.ppermute(xhead, "tx", DOWN)
    yp = lax.ppermute(yhead, "ty", DOWN)
    cmm = lax.ppermute(ym[:, tail], "tx", UP)
    cpm = lax.ppermute(xp[:, :, tail], "ty", UP)
    cpp = lax.ppermute(yp[:, head], "tx", DOWN)
    cmp = lax.ppermute(xm[:, :, head], "ty", DOWN)
    return xm, xp, ym, yp, cmm, cmp, cpm, cpp


def order_kernel(place, own_in, pair_in, core_in, diag_in, out, own, pair, core, diag, sems):
    copies = [
        pltpu.make_async_copy(src, dst, sems.at[i])
        for i, (src, dst) in enumerate(
            ((own_in, own), (pair_in, pair), (core_in, core), (diag_in, diag))
        )
    ]
    for copy in copies:
        copy.start()
    for copy in copies:
        copy.wait()
    lags, _, width = own.shape
    source = lax.broadcasted_iota(jnp.int32, (256, 512), 0)
    target = lax.broadcasted_iota(jnp.int32, (256, 512), 1)
    local = source % 128
    other_row = source // 128
    for lag in range(lags):
        for m in range(width // 128):
            cut = pl.ds(m * 128, 128)
            total = None
            for other_core, (a, b) in enumerate(((own, pair), (core, diag))):
                spot = (
                    (local // 16) * 64
                    + jnp.bitwise_xor(other_row, place[0]) * 32
                    + jnp.bitwise_xor(other_core, place[1]) * 16
                    + local % 16
                )
                hot = (spot == target).astype(F32).astype(BF16)
                both = jnp.concatenate([a[lag, :, cut], b[lag, :, cut]], axis=1)
                term = jnp.dot(both, hot, preferred_element_type=F32)
                total = term if total is None else total + term
            out[lag, :, pl.ds(m * 512, 512)] = total.astype(BF16)


def gathered_green(green):
    def moved(block, pairs):
        return lax.ppermute(block, "shot", pairs)

    pair = moved(green, PAIR_SWAP)
    core = moved(green, CORE_SWAP)
    diag = moved(pair, CORE_SWAP)
    me = lax.axis_index("shot")
    place = jnp.stack([me // 2 % 2, me % 2]).astype(jnp.int32)
    lags, points, width = green.shape
    vmem = pl.BlockSpec(memory_space=pltpu.VMEM)
    return pl.pallas_call(
        order_kernel,
        out_shape=jax.ShapeDtypeStruct((lags, points, 4 * width), BF16),
        in_specs=[pl.BlockSpec(memory_space=pltpu.SMEM)]
        + [pl.BlockSpec(memory_space=pltpu.HBM)] * 4,
        out_specs=vmem,
        scratch_shapes=[pltpu.VMEM(green.shape, BF16)] * 4 + [pltpu.SemaphoreType.DMA((4,))],
        compiler_params=pltpu.CompilerParams(vmem_limit_bytes=12 << 20),
        cost_estimate=pl.CostEstimate(flops=1_000_000_000, bytes_accessed=4_000_000, transcendentals=0),
        name="order",
    )(place, *in_hbm(green, pair, core, diag))


def block(
    wave_now, wave_prev, courant, rec_index, rec_history, green, lag_delay, emit_cells, emit_weights
):
    shots = wave_now.shape[0]
    receivers = rec_index.reshape(-1)
    rows_hot = (
        lax.shift_right_logical(receivers, 7)[:, None] == jnp.arange(TILE * TILE)[None, :]
    ).astype(BF16)
    lanes_hot = (
        jnp.bitwise_and(receivers, DEPTH - 1)[:, None] == jnp.arange(DEPTH)[None, :]
    ).astype(F32)
    halos = halo_blocks(wave_now, wave_prev, courant)
    wide_green = gathered_green(green)
    band = assemble(wave_now, wave_prev, courant, halos[:4])
    records, near, before = stencil(
        *band, halos[4:], rows_hot, lanes_hot, rec_history.reshape(shots * HIST, -1)
    )[:3]
    wave_last, field, cell_rows, cell_lanes = late(
        *in_hbm(near), before, courant, emit_cells.reshape(emit_cells.shape[-2:])
    )
    records = row_exchange(records)
    partial = columns(lag_delay, records, wide_green)
    partial = lax.all_to_all(partial.reshape(4, 512, 128), "tx", 0, 0, tiled=True)
    partial = jnp.sum(partial, axis=0).reshape(4, 2, 64, 128)
    partial = jnp.swapaxes(partial, 0, 1).reshape(8, 64, 128)
    partial = lax.all_to_all(
        partial, ("shot", "ty"), 0, 0, tiled=True, axis_index_groups=RING_GROUPS
    )
    summed = jnp.sum(partial.reshape(2, 4, 64, 128), axis=1)
    summed = jnp.swapaxes(summed.reshape(2, 4, 16, 128), 0, 1)
    em = lax.all_to_all(
        summed, "shot", 0, 0, tiled=True, axis_index_groups=COLUMN_GROUPS
    )
    wave_out, emission = inject(
        em, cell_rows, cell_lanes, emit_weights.reshape(emit_weights.shape[-2:]), field
    )
    return wave_out, wave_last, emission.reshape(shots, STEPS, 1, 1, -1)


def solution(mesh):
    return jax.shard_map(
        block,
        mesh=mesh,
        in_specs=(
            P("shot", "tx", "ty", None),
            P("shot", "tx", "ty", None),
            P("tx", "ty", None),
            P("tx", "ty", None),
            P("shot", None, "tx", "ty", None),
            P(None, ("tx", "ty"), "shot"),
            P(),
            P("tx", "ty", None, None),
            P("tx", "ty", None, None),
        ),
        out_specs=(
            P("shot", "tx", "ty", None),
            P("shot", "tx", "ty", None),
            P("shot", None, "tx", "ty", None),
        ),
        check_vma=False,
    )
```

```python
import jax
import jax.numpy as jnp
from jax import lax
from jax.experimental import pallas as pl
from jax.experimental.pallas import tpu as pltpu
from jax.sharding import PartitionSpec as P


STEPS = 8
HIST = 8
BAND = 8
TILE = 16
WIDE = TILE + 2 * BAND
DEPTH = 128
PAD = 8
F32 = jnp.float32
BF16 = jnp.bfloat16
NT = (((1,), (1,)), ((), ()))


def shot_id(half, row, core):
    return (half * 8 + row) * 2 + core


SHOT_COORDS = [(h, r, c) for h in range(2) for r in range(8) for c in range(2)]
CORE_SWAP = [(shot_id(h, r, c), shot_id(h, r, 1 - c)) for h, r, c in SHOT_COORDS]
PAIR_SWAP = [(shot_id(h, r, c), shot_id(h, r ^ 1, c)) for h, r, c in SHOT_COORDS]
ROW_GROUPS = [
    [shot_id(h, 2 * k + odd, c) for h in range(2) for k in range(4)]
    for odd in range(2)
    for c in range(2)
]
COLUMN_GROUPS = [
    [shot_id(h, 2 * k + odd, c) for k in range(4)]
    for h in range(2)
    for odd in range(2)
    for c in range(2)
]
RING_GROUPS = [
    [shot_id(h, r, c) * 4 + b for h in range(2) for b in range(4)] for r in range(8) for c in range(2)
]
UP = [(i, i + 1) for i in range(3)]
DOWN = [(i + 1, i) for i in range(3)]


def in_hbm(*arrays):
    return tuple(pltpu.with_memory_space_constraint(x, pltpu.HBM) for x in arrays)


def row_exchange(x):
    return lax.all_to_all(
        x, "shot", split_axis=0, concat_axis=0, tiled=True, axis_index_groups=ROW_GROUPS
    )


LOW = slice(0, BAND)
MID = slice(BAND, BAND + TILE)
HIGH = slice(BAND + TILE, WIDE)
YLOW = slice(PAD, PAD + BAND)
YMID = slice(PAD + BAND, PAD + BAND + TILE)
YHIGH = slice(PAD + BAND + TILE, PAD + WIDE)
HBM = pl.BlockSpec(memory_space=pltpu.HBM)
ANY = pl.BlockSpec(memory_space=pl.ANY)
VMEM = pl.BlockSpec(memory_space=pltpu.VMEM)


def band_copies(blocks, cur, prv, spd, sems):
    shots = cur.shape[0]
    copies = []
    for block, xs, ys in blocks:
        for src, dst in (
            (block.at[pl.ds(0, shots)], cur.at[:, xs, ys]),
            (block.at[pl.ds(shots, shots)], prv.at[:, xs, ys]),
            (block.at[2 * shots], spd.at[xs, ys]),
        ):
            copies.append(pltpu.make_async_copy(src, dst, sems.at[len(copies)]))
    return copies


def run(copies):
    for copy in copies:
        copy.start()
    for copy in copies:
        copy.wait()


def assemble_kernel(now, prev, speed, xm, xp, ym, yp, cur, prv, spd, own_sems, sems):
    own = [
        pltpu.make_async_copy(now, cur.at[:, MID, YMID], own_sems.at[0]),
        pltpu.make_async_copy(prev, prv.at[:, MID, YMID], own_sems.at[1]),
        pltpu.make_async_copy(speed, spd.at[MID, YMID], own_sems.at[2]),
    ]
    blocks = ((xm, LOW, YMID), (xp, HIGH, YMID), (ym, MID, YLOW), (yp, MID, YHIGH))
    run(own + band_copies(blocks, cur, prv, spd, sems))


def assemble(now, prev, speed, halos):
    shots = now.shape[0]
    wide = (shots, WIDE, WIDE + 2 * PAD, DEPTH)
    return pl.pallas_call(
        assemble_kernel,
        out_shape=(
            jax.ShapeDtypeStruct(wide, F32),
            jax.ShapeDtypeStruct(wide, F32),
            jax.ShapeDtypeStruct(wide[1:], F32),
        ),
        in_specs=[HBM] * 3 + [ANY] * 4,
        out_specs=(VMEM,) * 3,
        scratch_shapes=[pltpu.SemaphoreType.DMA((3,)), pltpu.SemaphoreType.DMA((12,))],
        compiler_params=pltpu.CompilerParams(vmem_limit_bytes=10 << 20),
        cost_estimate=pl.CostEstimate(flops=0, bytes_accessed=8_000_000, transcendentals=0),
        name="assemble",
    )(*in_hbm(now, prev, speed), *halos)


def advance(src, dst, spd, rows, start, count):
    lane = lax.broadcasted_iota(jnp.int32, (count, DEPTH), 1)

    def body(x, carry):
        cells = pl.ds(start, count)
        speed = spd[x, cells, :]
        centre = 2.0 - 6.0 * speed
        for s in range(src.shape[0]):
            u = src[s, x, pl.ds(start, count), :]
            total = src[s, x - 1, pl.ds(start, count), :] + src[s, x + 1, pl.ds(start, count), :]
            total = total + src[s, x, pl.ds(start - 1, count), :]
            total = total + src[s, x, pl.ds(start + 1, count), :]
            total = total + jnp.where(lane > 0, pltpu.roll(u, 1, 1), 0.0)
            total = total + jnp.where(lane < DEPTH - 1, pltpu.roll(u, DEPTH - 1, 1), 0.0)
            dst[s, x, cells, :] = centre * u - dst[s, x, cells, :] + speed * total
        return carry

    lax.fori_loop(*rows, body, 0, unroll=8)


def stencil_kernel(
    cur_in, prv_in, spd_in, cmm, cmp, cpm, cpp, rows_hot, lanes_hot, history,
    rec_out, next_out, last_out, cur, prv, spd, rec, sems, out_sems,
):
    shots = cur.shape[0]
    blocks = ((cmm, LOW, YLOW), (cmp, LOW, YHIGH), (cpm, HIGH, YLOW), (cpp, HIGH, YHIGH))
    run(band_copies(blocks, cur, prv, spd, sems))
    bufs = (cur, prv)
    sel_row = lax.broadcasted_iota(jnp.int32, (shots * STEPS, shots * DEPTH), 0)
    sel_col = lax.broadcasted_iota(jnp.int32, (shots * STEPS, shots * DEPTH), 1)
    mask = jnp.concatenate([lanes_hot[...]] * shots, axis=1)
    records = jnp.zeros((shots * STEPS, rows_hot.shape[0]), F32)
    for step in range(1, STEPS):
        src, dst = bufs[(step - 1) % 2], bufs[step % 2]
        start, count = (PAD, WIDE) if step < 4 else (PAD + 4, WIDE - 8)
        advance(src, dst, spd, (step, WIDE - step), start, count)
        field = jnp.concatenate(
            [dst[s, MID, YMID, :].reshape(TILE * TILE, DEPTH).astype(BF16) for s in range(shots)],
            axis=1,
        )
        picked = jnp.dot(rows_hot[...], field, preferred_element_type=F32)
        picked = (picked * mask).astype(BF16)
        sel = (sel_row == (sel_col // DEPTH) * STEPS + (step - 1)).astype(F32).astype(BF16)
        records = records + lax.dot_general(sel, picked, NT, preferred_element_type=F32)
    last = pltpu.make_async_copy(prv.at[:, MID, YMID], last_out, out_sems.at[8])
    last.start()
    advance(prv, cur, spd, (STEPS, WIDE - STEPS), PAD + BAND, TILE)
    rec[pl.ds(0, shots * HIST), :] = history[...]
    rec[pl.ds(shots * HIST, shots * STEPS), :] = records.astype(BF16)
    run(
        [pltpu.make_async_copy(rec, rec_out.at[g], out_sems.at[g]) for g in range(8)]
        + [pltpu.make_async_copy(cur.at[:, MID, YMID], next_out, out_sems.at[9])]
    )
    last.wait()


def stencil(cur, prv, spd, corners, rows_hot, lanes_hot, history):
    shots = cur.shape[0]
    points = rows_hot.shape[0]
    return pl.pallas_call(
        stencil_kernel,
        out_shape=(
            jax.ShapeDtypeStruct((8, shots * (HIST + STEPS), points), BF16),
            jax.ShapeDtypeStruct((shots, TILE, TILE, DEPTH), F32),
            jax.ShapeDtypeStruct((shots, TILE, TILE, DEPTH), F32),
            jax.ShapeDtypeStruct(cur.shape, F32),
            jax.ShapeDtypeStruct(cur.shape, F32),
            jax.ShapeDtypeStruct(spd.shape, F32),
        ),
        in_specs=[VMEM] * 3 + [ANY] * 4 + [VMEM] * 3,
        out_specs=(HBM,) * 3 + (VMEM,) * 3,
        input_output_aliases={0: 3, 1: 4, 2: 5},
        scratch_shapes=[
            pltpu.VMEM((shots * (HIST + STEPS), points), BF16),
            pltpu.SemaphoreType.DMA((12,)),
            pltpu.SemaphoreType.DMA((10,)),
        ],
        compiler_params=pltpu.CompilerParams(vmem_limit_bytes=20 << 20),
        cost_estimate=pl.CostEstimate(flops=2_000_000_000, bytes_accessed=12_000_000, transcendentals=0),
        name="stencil",
    )(cur, prv, spd, *corners, rows_hot, lanes_hot, history)


def columns_kernel(delay, records, green, out):
    groups, rows, _ = records.shape
    rows = rows // 2
    half = rows // 2
    lags = green.shape[0]
    width = green.shape[2]
    sel_row = lax.broadcasted_iota(jnp.int32, (half, 2 * rows), 0)
    sel_col = lax.broadcasted_iota(jnp.int32, (half, 2 * rows), 1)
    col_shot = (sel_col % rows) // STEPS
    col_time = (sel_col // rows) * HIST + sel_col % STEPS
    both = [records[g] for g in range(groups)]
    parts = []
    for h in range(2):
        row_shot = sel_row // STEPS + h * (half // STEPS)
        total = None
        for lag in range(lags):
            wanted = HIST + sel_row % STEPS - delay[lag]
            sel = jnp.logical_and(col_shot == row_shot, col_time == wanted)
            sel = sel.astype(F32).astype(BF16)
            window = jnp.concatenate(
                [jnp.dot(sel, b, preferred_element_type=F32).astype(BF16) for b in both], axis=0
            )
            term = jnp.dot(window, green[lag], preferred_element_type=F32)
            total = term if total is None else total + term
        parts.append(total)
    lane = lax.broadcasted_iota(jnp.int32, (groups * half, 128), 1)
    for m in range(width // 128):
        a = parts[0][:, m * 128 : (m + 1) * 128]
        b = parts[1][:, m * 128 : (m + 1) * 128]
        out[2 * m] = jnp.where(lane < 64, a, pltpu.roll(b, 64, 1))
        out[2 * m + 1] = jnp.where(lane < 64, pltpu.roll(a, 64, 1), b)


def columns(delay, records, green):
    vmem = pl.BlockSpec(memory_space=pltpu.VMEM)
    return pl.pallas_call(
        columns_kernel,
        out_shape=jax.ShapeDtypeStruct((16, 128, 128), F32),
        in_specs=[pl.BlockSpec(memory_space=pltpu.SMEM), vmem, vmem],
        out_specs=vmem,
        compiler_params=pltpu.CompilerParams(vmem_limit_bytes=12 << 20),
        cost_estimate=pl.CostEstimate(flops=1_000_000_000, bytes_accessed=4_000_000, transcendentals=0),
        name="columns",
    )(delay, records, green)


def inject_kernel(em, cells, weights, field, wave_out, emission_out, rhs_high, rhs_low, acc, emission):
    shots = field.shape[0]
    points = cells.shape[1]
    lane = lax.broadcasted_iota(jnp.int32, (16, 128), 1)
    for tile in range(4):
        even, odd = em[2 * tile % 4, tile // 2], em[2 * tile % 4 + 1, tile // 2]
        emission[pl.ds(0, 16), pl.ds(tile * 128, 128)] = jnp.where(lane < 64, even, pltpu.roll(odd, 64, 1))
        emission[pl.ds(16, 16), pl.ds(tile * 128, 128)] = jnp.where(lane < 64, pltpu.roll(even, 64, 1), odd)

    acc[...] = jnp.zeros_like(acc)
    row_iota = lax.broadcasted_iota(jnp.int32, (TILE * TILE, points), 0)
    lane_iota = lax.broadcasted_iota(jnp.int32, (DEPTH, points), 0)

    def body(k, carry):
        cell = cells[pl.ds(k, 1), :]
        weight = weights[pl.ds(k, 1), :]
        rows_hot = (row_iota == lax.shift_right_logical(cell, 7)).astype(F32).astype(BF16)
        lane_hot = lane_iota == jnp.bitwise_and(cell, DEPTH - 1)
        for s in range(shots):
            value = weight * emission[pl.ds(s * STEPS + STEPS - 1, 1), :]
            top = value.astype(BF16).astype(F32)
            rest = value - top
            rhs_high[pl.ds(s * DEPTH, DEPTH), :] = jnp.where(lane_hot, top, 0.0).astype(BF16)
            rhs_low[pl.ds(s * DEPTH, DEPTH), :] = jnp.where(lane_hot, rest, 0.0).astype(BF16)
        acc[...] += lax.dot_general(
            rows_hot, rhs_high[...], NT, preferred_element_type=F32
        ) + lax.dot_general(rows_hot, rhs_low[...], NT, preferred_element_type=F32)
        return carry

    lax.fori_loop(0, cells.shape[0], body, 0, unroll=4)
    for row in range(shots * STEPS):
        emission_out[row] = emission[pl.ds(row, 1), :]
    for s in range(shots):
        wave_out[s] = field[s] + acc[:, s * DEPTH : (s + 1) * DEPTH].reshape(TILE, TILE, DEPTH)


def inject(em, cells, weights, field):
    shots = field.shape[0]
    points = cells.shape[1]
    vmem = pl.BlockSpec(memory_space=pltpu.VMEM)
    return pl.pallas_call(
        inject_kernel,
        out_shape=(
            jax.ShapeDtypeStruct(field.shape, F32),
            jax.ShapeDtypeStruct((shots * STEPS, 1, points), F32),
        ),
        in_specs=[vmem] * 4,
        out_specs=(vmem, vmem),
        scratch_shapes=[
            pltpu.VMEM((shots * DEPTH, points), BF16),
            pltpu.VMEM((shots * DEPTH, points), BF16),
            pltpu.VMEM((TILE * TILE, shots * DEPTH), F32),
            pltpu.VMEM((shots * STEPS, points), F32),
        ],
        compiler_params=pltpu.CompilerParams(vmem_limit_bytes=12 << 20),
        cost_estimate=pl.CostEstimate(flops=4_000_000_000, bytes_accessed=4_000_000, transcendentals=0),
        name="inject",
    )(em, cells, weights, field)


def pack_kernel(now, prev, speed, xtail, ytail, xhead, yhead, sems):
    shots = now.shape[0]
    whole, head, tail = slice(None), slice(0, BAND), slice(TILE - BAND, TILE)
    copies = []
    for out, xs, ys in (
        (ytail, whole, tail), (xtail, tail, whole), (xhead, head, whole), (yhead, whole, head),
    ):
        for src, dst in (
            (now.at[:, xs, ys], out.at[pl.ds(0, shots)]),
            (prev.at[:, xs, ys], out.at[pl.ds(shots, shots)]),
            (speed.at[xs, ys], out.at[2 * shots]),
        ):
            copies.append(pltpu.make_async_copy(src, dst, sems.at[len(copies)]))
    run(copies)


def packed(now, prev, speed):
    fields = 2 * now.shape[0] + 1
    vmem = pl.BlockSpec(memory_space=pltpu.VMEM)
    across = jax.ShapeDtypeStruct((fields, BAND, TILE, DEPTH), F32)
    along = jax.ShapeDtypeStruct((fields, TILE, BAND, DEPTH), F32)
    return pl.pallas_call(
        pack_kernel,
        out_shape=(across, along, across, along),
        in_specs=[pl.BlockSpec(memory_space=pltpu.HBM)] * 3,
        out_specs=(vmem,) * 4,
        scratch_shapes=[pltpu.SemaphoreType.DMA((12,))],
        compiler_params=pltpu.CompilerParams(vmem_limit_bytes=8 << 20),
        cost_estimate=pl.CostEstimate(flops=0, bytes_accessed=4_000_000, transcendentals=0),
        name="pack",
    )(*in_hbm(now, prev, speed))


def halo_blocks(now, prev, speed):
    xtail, ytail, xhead, yhead = packed(now, prev, speed)
    head, tail = slice(0, BAND), slice(TILE - BAND, TILE)
    xm = lax.ppermute(xtail, "tx", UP)
    ym = lax.ppermute(ytail, "ty", UP)
    xp = lax.ppermute(xhead, "tx", DOWN)
    yp = lax.ppermute(yhead, "ty", DOWN)
    cmm = lax.ppermute(ym[:, tail], "tx", UP)
    cpm = lax.ppermute(xp[:, :, tail], "ty", UP)
    cpp = lax.ppermute(yp[:, head], "tx", DOWN)
    cmp = lax.ppermute(xm[:, :, head], "ty", DOWN)
    return xm, xp, ym, yp, cmm, cmp, cpm, cpp


def order_kernel(place, own_in, pair_in, core_in, diag_in, out, own, pair, core, diag, sems):
    copies = [
        pltpu.make_async_copy(src, dst, sems.at[i])
        for i, (src, dst) in enumerate(
            ((own_in, own), (pair_in, pair), (core_in, core), (diag_in, diag))
        )
    ]
    for copy in copies:
        copy.start()
    for copy in copies:
        copy.wait()
    lags, _, width = own.shape
    source = lax.broadcasted_iota(jnp.int32, (256, 512), 0)
    target = lax.broadcasted_iota(jnp.int32, (256, 512), 1)
    local = source % 128
    other_row = source // 128
    for lag in range(lags):
        for m in range(width // 128):
            cut = pl.ds(m * 128, 128)
            total = None
            for other_core, (a, b) in enumerate(((own, pair), (core, diag))):
                spot = (
                    (local // 16) * 64
                    + jnp.bitwise_xor(other_row, place[0]) * 32
                    + jnp.bitwise_xor(other_core, place[1]) * 16
                    + local % 16
                )
                hot = (spot == target).astype(F32).astype(BF16)
                both = jnp.concatenate([a[lag, :, cut], b[lag, :, cut]], axis=1)
                term = jnp.dot(both, hot, preferred_element_type=F32)
                total = term if total is None else total + term
            out[lag, :, pl.ds(m * 512, 512)] = total.astype(BF16)


def gathered_green(green):
    def moved(block, pairs):
        return lax.ppermute(block, "shot", pairs)

    pair = moved(green, PAIR_SWAP)
    core = moved(green, CORE_SWAP)
    diag = moved(pair, CORE_SWAP)
    me = lax.axis_index("shot")
    place = jnp.stack([me // 2 % 2, me % 2]).astype(jnp.int32)
    lags, points, width = green.shape
    vmem = pl.BlockSpec(memory_space=pltpu.VMEM)
    return pl.pallas_call(
        order_kernel,
        out_shape=jax.ShapeDtypeStruct((lags, points, 4 * width), BF16),
        in_specs=[pl.BlockSpec(memory_space=pltpu.SMEM)]
        + [pl.BlockSpec(memory_space=pltpu.HBM)] * 4,
        out_specs=vmem,
        scratch_shapes=[pltpu.VMEM(green.shape, BF16)] * 4 + [pltpu.SemaphoreType.DMA((4,))],
        compiler_params=pltpu.CompilerParams(vmem_limit_bytes=12 << 20),
        cost_estimate=pl.CostEstimate(flops=1_000_000_000, bytes_accessed=4_000_000, transcendentals=0),
        name="order",
    )(place, *in_hbm(green, pair, core, diag))


def block(
    wave_now, wave_prev, courant, rec_index, rec_history, green, lag_delay, emit_cells, emit_weights
):
    shots = wave_now.shape[0]
    receivers = rec_index.reshape(-1)
    rows_hot = (
        lax.shift_right_logical(receivers, 7)[:, None] == jnp.arange(TILE * TILE)[None, :]
    ).astype(BF16)
    lanes_hot = (
        jnp.bitwise_and(receivers, DEPTH - 1)[:, None] == jnp.arange(DEPTH)[None, :]
    ).astype(F32)
    halos = halo_blocks(wave_now, wave_prev, courant)
    wide_green = gathered_green(green)
    band = assemble(wave_now, wave_prev, courant, halos[:4])
    records, field, wave_last = stencil(
        *band, halos[4:], rows_hot, lanes_hot, rec_history.reshape(shots * HIST, -1)
    )[:3]
    records = row_exchange(records)
    partial = columns(lag_delay, records, wide_green)
    partial = lax.all_to_all(partial.reshape(4, 512, 128), "tx", 0, 0, tiled=True)
    partial = jnp.sum(partial, axis=0).reshape(4, 2, 64, 128)
    partial = jnp.swapaxes(partial, 0, 1).reshape(8, 64, 128)
    partial = lax.all_to_all(
        partial, ("shot", "ty"), 0, 0, tiled=True, axis_index_groups=RING_GROUPS
    )
    summed = jnp.sum(partial.reshape(2, 4, 64, 128), axis=1)
    summed = jnp.swapaxes(summed.reshape(2, 4, 16, 128), 0, 1)
    em = lax.all_to_all(
        summed, "shot", 0, 0, tiled=True, axis_index_groups=COLUMN_GROUPS
    )
    wave_out, emission = inject(
        em, emit_cells.reshape(emit_cells.shape[-2:]), emit_weights.reshape(emit_weights.shape[-2:]), field
    )
    return wave_out, wave_last, emission.reshape(shots, STEPS, 1, 1, -1)


def solution(mesh):
    return jax.shard_map(
        block,
        mesh=mesh,
        in_specs=(
            P("shot", "tx", "ty", None),
            P("shot", "tx", "ty", None),
            P("tx", "ty", None),
            P("tx", "ty", None),
            P("shot", None, "tx", "ty", None),
            P(None, ("tx", "ty"), "shot"),
            P(),
            P("tx", "ty", None, None),
            P("tx", "ty", None, None),
        ),
        out_specs=(
            P("shot", "tx", "ty", None),
            P("shot", "tx", "ty", None),
            P("shot", None, "tx", "ty", None),
        ),
        check_vma=False,
    )
```

```python
import jax
import jax.numpy as jnp
from jax import lax
from jax.experimental import pallas as pl
from jax.experimental.pallas import tpu as pltpu
from jax.sharding import PartitionSpec as P


STEPS = 8
HIST = 8
BAND = 8
TILE = 16
WIDE = TILE + 2 * BAND
DEPTH = 128
PAD = 8
F32 = jnp.float32
BF16 = jnp.bfloat16
NT = (((1,), (1,)), ((), ()))


def shot_id(half, row, core):
    return (half * 8 + row) * 2 + core


SHOT_COORDS = [(h, r, c) for h in range(2) for r in range(8) for c in range(2)]
CORE_SWAP = [(shot_id(h, r, c), shot_id(h, r, 1 - c)) for h, r, c in SHOT_COORDS]
PAIR_SWAP = [(shot_id(h, r, c), shot_id(h, r ^ 1, c)) for h, r, c in SHOT_COORDS]
ROW_GROUPS = [
    [shot_id(h, 2 * k + odd, c) for h in range(2) for k in range(4)]
    for odd in range(2)
    for c in range(2)
]
COLUMN_GROUPS = [
    [shot_id(h, 2 * k + odd, c) for k in range(4)]
    for h in range(2)
    for odd in range(2)
    for c in range(2)
]
RING_GROUPS = [
    [shot_id(h, r, c) * 4 + b for h in range(2) for b in range(4)] for r in range(8) for c in range(2)
]
UP = [(i, i + 1) for i in range(3)]
DOWN = [(i + 1, i) for i in range(3)]


def in_hbm(*arrays):
    return tuple(pltpu.with_memory_space_constraint(x, pltpu.HBM) for x in arrays)


def row_exchange(x):
    return lax.all_to_all(
        x, "shot", split_axis=0, concat_axis=0, tiled=True, axis_index_groups=ROW_GROUPS
    )


LOW = slice(0, BAND)
MID = slice(BAND, BAND + TILE)
HIGH = slice(BAND + TILE, WIDE)
YLOW = slice(PAD, PAD + BAND)
YMID = slice(PAD + BAND, PAD + BAND + TILE)
YHIGH = slice(PAD + BAND + TILE, PAD + WIDE)
HBM = pl.BlockSpec(memory_space=pltpu.HBM)
ANY = pl.BlockSpec(memory_space=pl.ANY)
VMEM = pl.BlockSpec(memory_space=pltpu.VMEM)


def band_copies(blocks, cur, prv, spd, sems):
    shots = cur.shape[0]
    copies = []
    for block, xs, ys in blocks:
        for src, dst in (
            (block.at[pl.ds(0, shots)], cur.at[:, xs, ys]),
            (block.at[pl.ds(shots, shots)], prv.at[:, xs, ys]),
            (block.at[2 * shots], spd.at[xs, ys]),
        ):
            copies.append(pltpu.make_async_copy(src, dst, sems.at[len(copies)]))
    return copies


def run(copies):
    for copy in copies:
        copy.start()
    for copy in copies:
        copy.wait()


def assemble_kernel(now, prev, speed, xm, xp, ym, yp, cur, prv, spd, own_sems, sems):
    own = [
        pltpu.make_async_copy(now, cur.at[:, MID, YMID], own_sems.at[0]),
        pltpu.make_async_copy(prev, prv.at[:, MID, YMID], own_sems.at[1]),
        pltpu.make_async_copy(speed, spd.at[MID, YMID], own_sems.at[2]),
    ]
    blocks = ((xm, LOW, YMID), (xp, HIGH, YMID), (ym, MID, YLOW), (yp, MID, YHIGH))
    run(own + band_copies(blocks, cur, prv, spd, sems))


def assemble(now, prev, speed, halos):
    shots = now.shape[0]
    wide = (shots, WIDE, WIDE + 2 * PAD, DEPTH)
    return pl.pallas_call(
        assemble_kernel,
        out_shape=(
            jax.ShapeDtypeStruct(wide, F32),
            jax.ShapeDtypeStruct(wide, F32),
            jax.ShapeDtypeStruct(wide[1:], F32),
        ),
        in_specs=[HBM] * 3 + [ANY] * 4,
        out_specs=(VMEM,) * 3,
        scratch_shapes=[pltpu.SemaphoreType.DMA((3,)), pltpu.SemaphoreType.DMA((12,))],
        compiler_params=pltpu.CompilerParams(vmem_limit_bytes=10 << 20),
        cost_estimate=pl.CostEstimate(flops=0, bytes_accessed=8_000_000, transcendentals=0),
        name="assemble",
    )(*in_hbm(now, prev, speed), *halos)


def advance(src, dst, spd, rows, start, count):
    lane = lax.broadcasted_iota(jnp.int32, (count, DEPTH), 1)

    def body(x, carry):
        cells = pl.ds(start, count)
        speed = spd[x, cells, :]
        centre = 2.0 - 6.0 * speed
        for s in range(src.shape[0]):
            u = src[s, x, pl.ds(start, count), :]
            total = src[s, x - 1, pl.ds(start, count), :] + src[s, x + 1, pl.ds(start, count), :]
            total = total + src[s, x, pl.ds(start - 1, count), :]
            total = total + src[s, x, pl.ds(start + 1, count), :]
            total = total + jnp.where(lane > 0, pltpu.roll(u, 1, 1), 0.0)
            total = total + jnp.where(lane < DEPTH - 1, pltpu.roll(u, DEPTH - 1, 1), 0.0)
            dst[s, x, cells, :] = centre * u - dst[s, x, cells, :] + speed * total
        return carry

    lax.fori_loop(*rows, body, 0, unroll=8)


def stencil_kernel(
    cur_in, prv_in, spd_in, cmm, cmp, cpm, cpp, rows_hot, lanes_hot, history,
    rec_out, next_out, last_out, cur, prv, spd, rec, sems, out_sems,
):
    shots = cur.shape[0]
    blocks = ((cmm, LOW, YLOW), (cmp, LOW, YHIGH), (cpm, HIGH, YLOW), (cpp, HIGH, YHIGH))
    run(band_copies(blocks, cur, prv, spd, sems))
    bufs = (cur, prv)
    sel_row = lax.broadcasted_iota(jnp.int32, (shots * STEPS, shots * DEPTH), 0)
    sel_col = lax.broadcasted_iota(jnp.int32, (shots * STEPS, shots * DEPTH), 1)
    mask = jnp.concatenate([lanes_hot[...]] * shots, axis=1)
    records = jnp.zeros((shots * STEPS, rows_hot.shape[0]), F32)
    for step in range(1, STEPS):
        src, dst = bufs[(step - 1) % 2], bufs[step % 2]
        start, count = (PAD, WIDE) if step < 4 else (PAD + 4, WIDE - 8)
        advance(src, dst, spd, (step, WIDE - step), start, count)
        field = jnp.concatenate(
            [dst[s, MID, YMID, :].reshape(TILE * TILE, DEPTH).astype(BF16) for s in range(shots)],
            axis=1,
        )
        picked = jnp.dot(rows_hot[...], field, preferred_element_type=F32)
        picked = (picked * mask).astype(BF16)
        sel = (sel_row == (sel_col // DEPTH) * STEPS + (step - 1)).astype(F32).astype(BF16)
        records = records + lax.dot_general(sel, picked, NT, preferred_element_type=F32)
    last = pltpu.make_async_copy(prv.at[:, MID, YMID], last_out, out_sems.at[8])
    last.start()
    advance(prv, cur, spd, (STEPS, WIDE - STEPS), PAD + BAND, TILE)
    rec[pl.ds(0, shots * HIST), :] = history[...]
    rec[pl.ds(shots * HIST, shots * STEPS), :] = records.astype(BF16)
    run(
        [pltpu.make_async_copy(rec, rec_out.at[g], out_sems.at[g]) for g in range(8)]
        + [pltpu.make_async_copy(cur.at[:, MID, YMID], next_out, out_sems.at[9])]
    )
    last.wait()


def stencil(cur, prv, spd, corners, rows_hot, lanes_hot, history):
    shots = cur.shape[0]
    points = rows_hot.shape[0]
    return pl.pallas_call(
        stencil_kernel,
        out_shape=(
            jax.ShapeDtypeStruct((8, shots * (HIST + STEPS), points), BF16),
            jax.ShapeDtypeStruct((shots, TILE, TILE, DEPTH), F32),
            jax.ShapeDtypeStruct((shots, TILE, TILE, DEPTH), F32),
            jax.ShapeDtypeStruct(cur.shape, F32),
            jax.ShapeDtypeStruct(cur.shape, F32),
            jax.ShapeDtypeStruct(spd.shape, F32),
        ),
        in_specs=[VMEM] * 3 + [ANY] * 4 + [VMEM] * 3,
        out_specs=(HBM,) * 3 + (VMEM,) * 3,
        input_output_aliases={0: 3, 1: 4, 2: 5},
        scratch_shapes=[
            pltpu.VMEM((shots * (HIST + STEPS), points), BF16),
            pltpu.SemaphoreType.DMA((12,)),
            pltpu.SemaphoreType.DMA((10,)),
        ],
        compiler_params=pltpu.CompilerParams(vmem_limit_bytes=20 << 20),
        cost_estimate=pl.CostEstimate(flops=2_000_000_000, bytes_accessed=12_000_000, transcendentals=0),
        name="stencil",
    )(cur, prv, spd, *corners, rows_hot, lanes_hot, history)


def columns_kernel(delay, records, green, out):
    groups, rows, _ = records.shape
    rows = rows // 2
    half = rows // 2
    lags = green.shape[0]
    width = green.shape[2]
    sel_row = lax.broadcasted_iota(jnp.int32, (half, 2 * rows), 0)
    sel_col = lax.broadcasted_iota(jnp.int32, (half, 2 * rows), 1)
    col_shot = (sel_col % rows) // STEPS
    col_time = (sel_col // rows) * HIST + sel_col % STEPS
    both = [records[g] for g in range(groups)]
    parts = []
    for h in range(2):
        row_shot = sel_row // STEPS + h * (half // STEPS)
        total = None
        for lag in range(lags):
            wanted = HIST + sel_row % STEPS - delay[lag]
            sel = jnp.logical_and(col_shot == row_shot, col_time == wanted)
            sel = sel.astype(F32).astype(BF16)
            window = jnp.concatenate(
                [jnp.dot(sel, b, preferred_element_type=F32).astype(BF16) for b in both], axis=0
            )
            term = jnp.dot(window, green[lag], preferred_element_type=F32)
            total = term if total is None else total + term
        parts.append(total)
    lane = lax.broadcasted_iota(jnp.int32, (groups * half, 128), 1)
    for m in range(width // 128):
        a = parts[0][:, m * 128 : (m + 1) * 128]
        b = parts[1][:, m * 128 : (m + 1) * 128]
        out[2 * m] = jnp.where(lane < 64, a, pltpu.roll(b, 64, 1)).astype(BF16)
        out[2 * m + 1] = jnp.where(lane < 64, pltpu.roll(a, 64, 1), b).astype(BF16)


def columns(delay, records, green):
    vmem = pl.BlockSpec(memory_space=pltpu.VMEM)
    return pl.pallas_call(
        columns_kernel,
        out_shape=jax.ShapeDtypeStruct((16, 128, 128), BF16),
        in_specs=[pl.BlockSpec(memory_space=pltpu.SMEM), vmem, vmem],
        out_specs=vmem,
        compiler_params=pltpu.CompilerParams(vmem_limit_bytes=12 << 20),
        cost_estimate=pl.CostEstimate(flops=1_000_000_000, bytes_accessed=4_000_000, transcendentals=0),
        name="columns",
    )(delay, records, green)


def inject_kernel(em, cells, weights, field, wave_out, emission_out, rhs_high, rhs_low, acc, emission):
    shots = field.shape[0]
    points = cells.shape[1]
    lane = lax.broadcasted_iota(jnp.int32, (16, 128), 1)
    for tile in range(4):
        even, odd = em[2 * tile % 4, tile // 2], em[2 * tile % 4 + 1, tile // 2]
        emission[pl.ds(0, 16), pl.ds(tile * 128, 128)] = jnp.where(lane < 64, even, pltpu.roll(odd, 64, 1))
        emission[pl.ds(16, 16), pl.ds(tile * 128, 128)] = jnp.where(lane < 64, pltpu.roll(even, 64, 1), odd)

    acc[...] = jnp.zeros_like(acc)
    row_iota = lax.broadcasted_iota(jnp.int32, (TILE * TILE, points), 0)
    lane_iota = lax.broadcasted_iota(jnp.int32, (DEPTH, points), 0)

    def body(k, carry):
        cell = cells[pl.ds(k, 1), :]
        weight = weights[pl.ds(k, 1), :]
        rows_hot = (row_iota == lax.shift_right_logical(cell, 7)).astype(F32).astype(BF16)
        lane_hot = lane_iota == jnp.bitwise_and(cell, DEPTH - 1)
        for s in range(shots):
            value = weight * emission[pl.ds(s * STEPS + STEPS - 1, 1), :]
            top = value.astype(BF16).astype(F32)
            rest = value - top
            rhs_high[pl.ds(s * DEPTH, DEPTH), :] = jnp.where(lane_hot, top, 0.0).astype(BF16)
            rhs_low[pl.ds(s * DEPTH, DEPTH), :] = jnp.where(lane_hot, rest, 0.0).astype(BF16)
        acc[...] += lax.dot_general(
            rows_hot, rhs_high[...], NT, preferred_element_type=F32
        ) + lax.dot_general(rows_hot, rhs_low[...], NT, preferred_element_type=F32)
        return carry

    lax.fori_loop(0, cells.shape[0], body, 0, unroll=4)
    for row in range(shots * STEPS):
        emission_out[row] = emission[pl.ds(row, 1), :]
    for s in range(shots):
        wave_out[s] = field[s] + acc[:, s * DEPTH : (s + 1) * DEPTH].reshape(TILE, TILE, DEPTH)


def inject(em, cells, weights, field):
    shots = field.shape[0]
    points = cells.shape[1]
    vmem = pl.BlockSpec(memory_space=pltpu.VMEM)
    return pl.pallas_call(
        inject_kernel,
        out_shape=(
            jax.ShapeDtypeStruct(field.shape, F32),
            jax.ShapeDtypeStruct((shots * STEPS, 1, points), F32),
        ),
        in_specs=[vmem] * 4,
        out_specs=(vmem, vmem),
        scratch_shapes=[
            pltpu.VMEM((shots * DEPTH, points), BF16),
            pltpu.VMEM((shots * DEPTH, points), BF16),
            pltpu.VMEM((TILE * TILE, shots * DEPTH), F32),
            pltpu.VMEM((shots * STEPS, points), F32),
        ],
        compiler_params=pltpu.CompilerParams(vmem_limit_bytes=12 << 20),
        cost_estimate=pl.CostEstimate(flops=4_000_000_000, bytes_accessed=4_000_000, transcendentals=0),
        name="inject",
    )(em, cells, weights, field)


def pack_kernel(now, prev, speed, xtail, ytail, xhead, yhead, field, sems):
    shots = now.shape[0]
    copies = [
        pltpu.make_async_copy(now, field.at[pl.ds(0, shots)], sems.at[0]),
        pltpu.make_async_copy(prev, field.at[pl.ds(shots, shots)], sems.at[1]),
        pltpu.make_async_copy(speed, field.at[2 * shots], sems.at[2]),
    ]
    for copy in copies:
        copy.start()
    for copy in copies:
        copy.wait()
    head, tail = slice(0, BAND), slice(TILE - BAND, TILE)
    xtail[...] = field[:, tail]
    ytail[...] = field[:, :, tail]
    xhead[...] = field[:, head]
    yhead[...] = field[:, :, head]


def packed(now, prev, speed):
    fields = 2 * now.shape[0] + 1
    vmem = pl.BlockSpec(memory_space=pltpu.VMEM)
    across = jax.ShapeDtypeStruct((fields, BAND, TILE, DEPTH), F32)
    along = jax.ShapeDtypeStruct((fields, TILE, BAND, DEPTH), F32)
    return pl.pallas_call(
        pack_kernel,
        out_shape=(across, along, across, along),
        in_specs=[pl.BlockSpec(memory_space=pltpu.HBM)] * 3,
        out_specs=(vmem,) * 4,
        scratch_shapes=[
            pltpu.VMEM((fields, TILE, TILE, DEPTH), F32),
            pltpu.SemaphoreType.DMA((3,)),
        ],
        compiler_params=pltpu.CompilerParams(vmem_limit_bytes=8 << 20),
        cost_estimate=pl.CostEstimate(flops=0, bytes_accessed=4_000_000, transcendentals=0),
        name="pack",
    )(*in_hbm(now, prev, speed))


def halo_blocks(now, prev, speed):
    xtail, ytail, xhead, yhead = packed(now, prev, speed)
    head, tail = slice(0, BAND), slice(TILE - BAND, TILE)
    xm = lax.ppermute(xtail, "tx", UP)
    ym = lax.ppermute(ytail, "ty", UP)
    xp = lax.ppermute(xhead, "tx", DOWN)
    yp = lax.ppermute(yhead, "ty", DOWN)
    cmm = lax.ppermute(ym[:, tail], "tx", UP)
    cpm = lax.ppermute(xp[:, :, tail], "ty", UP)
    cpp = lax.ppermute(yp[:, head], "tx", DOWN)
    cmp = lax.ppermute(xm[:, :, head], "ty", DOWN)
    return xm, xp, ym, yp, cmm, cmp, cpm, cpp


def order_kernel(place, own_in, pair_in, core_in, diag_in, out, own, pair, core, diag, sems):
    copies = [
        pltpu.make_async_copy(src, dst, sems.at[i])
        for i, (src, dst) in enumerate(
            ((own_in, own), (pair_in, pair), (core_in, core), (diag_in, diag))
        )
    ]
    for copy in copies:
        copy.start()
    for copy in copies:
        copy.wait()
    lags, _, width = own.shape
    source = lax.broadcasted_iota(jnp.int32, (256, 512), 0)
    target = lax.broadcasted_iota(jnp.int32, (256, 512), 1)
    local = source % 128
    other_row = source // 128
    for lag in range(lags):
        for m in range(width // 128):
            cut = pl.ds(m * 128, 128)
            total = None
            for other_core, (a, b) in enumerate(((own, pair), (core, diag))):
                spot = (
                    (local // 16) * 64
                    + jnp.bitwise_xor(other_row, place[0]) * 32
                    + jnp.bitwise_xor(other_core, place[1]) * 16
                    + local % 16
                )
                hot = (spot == target).astype(F32).astype(BF16)
                both = jnp.concatenate([a[lag, :, cut], b[lag, :, cut]], axis=1)
                term = jnp.dot(both, hot, preferred_element_type=F32)
                total = term if total is None else total + term
            out[lag, :, pl.ds(m * 512, 512)] = total.astype(BF16)


def gathered_green(green):
    def moved(block, pairs):
        return lax.ppermute(block, "shot", pairs)

    pair = moved(green, PAIR_SWAP)
    core = moved(green, CORE_SWAP)
    diag = moved(pair, CORE_SWAP)
    me = lax.axis_index("shot")
    place = jnp.stack([me // 2 % 2, me % 2]).astype(jnp.int32)
    lags, points, width = green.shape
    vmem = pl.BlockSpec(memory_space=pltpu.VMEM)
    return pl.pallas_call(
        order_kernel,
        out_shape=jax.ShapeDtypeStruct((lags, points, 4 * width), BF16),
        in_specs=[pl.BlockSpec(memory_space=pltpu.SMEM)]
        + [pl.BlockSpec(memory_space=pltpu.HBM)] * 4,
        out_specs=vmem,
        scratch_shapes=[pltpu.VMEM(green.shape, BF16)] * 4 + [pltpu.SemaphoreType.DMA((4,))],
        compiler_params=pltpu.CompilerParams(vmem_limit_bytes=12 << 20),
        cost_estimate=pl.CostEstimate(flops=1_000_000_000, bytes_accessed=4_000_000, transcendentals=0),
        name="order",
    )(place, *in_hbm(green, pair, core, diag))


def block(
    wave_now, wave_prev, courant, rec_index, rec_history, green, lag_delay, emit_cells, emit_weights
):
    shots = wave_now.shape[0]
    receivers = rec_index.reshape(-1)
    rows_hot = (
        lax.shift_right_logical(receivers, 7)[:, None] == jnp.arange(TILE * TILE)[None, :]
    ).astype(BF16)
    lanes_hot = (
        jnp.bitwise_and(receivers, DEPTH - 1)[:, None] == jnp.arange(DEPTH)[None, :]
    ).astype(F32)
    halos = halo_blocks(wave_now, wave_prev, courant)
    wide_green = gathered_green(green)
    band = assemble(wave_now, wave_prev, courant, halos[:4])
    records, field, wave_last = stencil(
        *band, halos[4:], rows_hot, lanes_hot, rec_history.reshape(shots * HIST, -1)
    )[:3]
    records = row_exchange(records)
    partial = columns(lag_delay, records, wide_green)
    partial = lax.all_to_all(partial.reshape(4, 512, 128), "tx", 0, 0, tiled=True)
    partial = jnp.sum(partial.astype(F32), axis=0).reshape(4, 2, 64, 128)
    partial = jnp.swapaxes(partial, 0, 1).reshape(8, 64, 128)
    partial = lax.all_to_all(
        partial, ("shot", "ty"), 0, 0, tiled=True, axis_index_groups=RING_GROUPS
    )
    summed = jnp.sum(partial.reshape(2, 4, 64, 128), axis=1)
    summed = jnp.swapaxes(summed.reshape(2, 4, 16, 128), 0, 1)
    em = lax.all_to_all(
        summed, "shot", 0, 0, tiled=True, axis_index_groups=COLUMN_GROUPS
    )
    wave_out, emission = inject(
        em, emit_cells.reshape(emit_cells.shape[-2:]), emit_weights.reshape(emit_weights.shape[-2:]), field
    )
    return wave_out, wave_last, emission.reshape(shots, STEPS, 1, 1, -1)


def solution(mesh):
    return jax.shard_map(
        block,
        mesh=mesh,
        in_specs=(
            P("shot", "tx", "ty", None),
            P("shot", "tx", "ty", None),
            P("tx", "ty", None),
            P("tx", "ty", None),
            P("shot", None, "tx", "ty", None),
            P(None, ("tx", "ty"), "shot"),
            P(),
            P("tx", "ty", None, None),
            P("tx", "ty", None, None),
        ),
        out_specs=(
            P("shot", "tx", "ty", None),
            P("shot", "tx", "ty", None),
            P("shot", None, "tx", "ty", None),
        ),
        check_vma=False,
    )
```

```python
import jax
import jax.numpy as jnp
from jax import lax
from jax.experimental import pallas as pl
from jax.experimental.pallas import tpu as pltpu
from jax.sharding import PartitionSpec as P


STEPS = 8
HIST = 8
BAND = 8
TILE = 16
WIDE = TILE + 2 * BAND
DEPTH = 128
PAD = 8
F32 = jnp.float32
BF16 = jnp.bfloat16
NT = (((1,), (1,)), ((), ()))


def shot_id(half, row, core):
    return (half * 8 + row) * 2 + core


SHOT_COORDS = [(h, r, c) for h in range(2) for r in range(8) for c in range(2)]
CORE_SWAP = [(shot_id(h, r, c), shot_id(h, r, 1 - c)) for h, r, c in SHOT_COORDS]
PAIR_SWAP = [(shot_id(h, r, c), shot_id(h, r ^ 1, c)) for h, r, c in SHOT_COORDS]
ROW_GROUPS = [
    [shot_id(h, 2 * k + odd, c) for h in range(2) for k in range(4)]
    for odd in range(2)
    for c in range(2)
]
UP = [(i, i + 1) for i in range(3)]
DOWN = [(i + 1, i) for i in range(3)]


def in_hbm(*arrays):
    return tuple(pltpu.with_memory_space_constraint(x, pltpu.HBM) for x in arrays)


def row_exchange(x):
    return lax.all_to_all(
        x, "shot", split_axis=0, concat_axis=0, tiled=True, axis_index_groups=ROW_GROUPS
    )


LOW = slice(0, BAND)
MID = slice(BAND, BAND + TILE)
HIGH = slice(BAND + TILE, WIDE)
YLOW = slice(PAD, PAD + BAND)
YMID = slice(PAD + BAND, PAD + BAND + TILE)
YHIGH = slice(PAD + BAND + TILE, PAD + WIDE)
HBM = pl.BlockSpec(memory_space=pltpu.HBM)
ANY = pl.BlockSpec(memory_space=pl.ANY)
VMEM = pl.BlockSpec(memory_space=pltpu.VMEM)


def band_copies(blocks, cur, prv, spd, sems):
    shots = cur.shape[0]
    copies = []
    for block, xs, ys in blocks:
        for src, dst in (
            (block.at[pl.ds(0, shots)], cur.at[:, xs, ys]),
            (block.at[pl.ds(shots, shots)], prv.at[:, xs, ys]),
            (block.at[2 * shots], spd.at[xs, ys]),
        ):
            copies.append(pltpu.make_async_copy(src, dst, sems.at[len(copies)]))
    return copies


def run(copies):
    for copy in copies:
        copy.start()
    for copy in copies:
        copy.wait()


def assemble_kernel(now, prev, speed, xm, xp, ym, yp, cur, prv, spd, own_sems, sems):
    own = [
        pltpu.make_async_copy(now, cur.at[:, MID, YMID], own_sems.at[0]),
        pltpu.make_async_copy(prev, prv.at[:, MID, YMID], own_sems.at[1]),
        pltpu.make_async_copy(speed, spd.at[MID, YMID], own_sems.at[2]),
    ]
    blocks = ((xm, LOW, YMID), (xp, HIGH, YMID), (ym, MID, YLOW), (yp, MID, YHIGH))
    run(own + band_copies(blocks, cur, prv, spd, sems))


def assemble(now, prev, speed, halos):
    shots = now.shape[0]
    wide = (shots, WIDE, WIDE + 2 * PAD, DEPTH)
    return pl.pallas_call(
        assemble_kernel,
        out_shape=(
            jax.ShapeDtypeStruct(wide, F32),
            jax.ShapeDtypeStruct(wide, F32),
            jax.ShapeDtypeStruct(wide[1:], F32),
        ),
        in_specs=[HBM] * 3 + [ANY] * 4,
        out_specs=(VMEM,) * 3,
        scratch_shapes=[pltpu.SemaphoreType.DMA((3,)), pltpu.SemaphoreType.DMA((12,))],
        compiler_params=pltpu.CompilerParams(vmem_limit_bytes=10 << 20),
        cost_estimate=pl.CostEstimate(flops=0, bytes_accessed=8_000_000, transcendentals=0),
        name="assemble",
    )(*in_hbm(now, prev, speed), *halos)


def advance(src, dst, spd, rows, start, count):
    lane = lax.broadcasted_iota(jnp.int32, (count, DEPTH), 1)

    def body(x, carry):
        cells = pl.ds(start, count)
        speed = spd[x, cells, :]
        centre = 2.0 - 6.0 * speed
        for s in range(src.shape[0]):
            u = src[s, x, pl.ds(start, count), :]
            total = src[s, x - 1, pl.ds(start, count), :] + src[s, x + 1, pl.ds(start, count), :]
            total = total + src[s, x, pl.ds(start - 1, count), :]
            total = total + src[s, x, pl.ds(start + 1, count), :]
            total = total + jnp.where(lane > 0, pltpu.roll(u, 1, 1), 0.0)
            total = total + jnp.where(lane < DEPTH - 1, pltpu.roll(u, DEPTH - 1, 1), 0.0)
            dst[s, x, cells, :] = centre * u - dst[s, x, cells, :] + speed * total
        return carry

    lax.fori_loop(*rows, body, 0, unroll=8)


def stencil_kernel(
    cur_in, prv_in, spd_in, cmm, cmp, cpm, cpp, rows_hot, lanes_hot, history,
    rec_out, next_out, last_out, cur, prv, spd, rec, sems, out_sems,
):
    shots = cur.shape[0]
    blocks = ((cmm, LOW, YLOW), (cmp, LOW, YHIGH), (cpm, HIGH, YLOW), (cpp, HIGH, YHIGH))
    run(band_copies(blocks, cur, prv, spd, sems))
    bufs = (cur, prv)
    sel_row = lax.broadcasted_iota(jnp.int32, (shots * STEPS, shots * DEPTH), 0)
    sel_col = lax.broadcasted_iota(jnp.int32, (shots * STEPS, shots * DEPTH), 1)
    mask = jnp.concatenate([lanes_hot[...]] * shots, axis=1)
    records = jnp.zeros((shots * STEPS, rows_hot.shape[0]), F32)
    for step in range(1, STEPS):
        src, dst = bufs[(step - 1) % 2], bufs[step % 2]
        start, count = (PAD, WIDE) if step < 4 else (PAD + 4, WIDE - 8)
        advance(src, dst, spd, (step, WIDE - step), start, count)
        field = jnp.concatenate(
            [dst[s, MID, YMID, :].reshape(TILE * TILE, DEPTH).astype(BF16) for s in range(shots)],
            axis=1,
        )
        picked = jnp.dot(rows_hot[...], field, preferred_element_type=F32)
        picked = (picked * mask).astype(BF16)
        sel = (sel_row == (sel_col // DEPTH) * STEPS + (step - 1)).astype(F32).astype(BF16)
        records = records + lax.dot_general(sel, picked, NT, preferred_element_type=F32)
    last = pltpu.make_async_copy(prv.at[:, MID, YMID], last_out, out_sems.at[8])
    last.start()
    advance(prv, cur, spd, (STEPS, WIDE - STEPS), PAD + BAND, TILE)
    rec[pl.ds(0, shots * HIST), :] = history[...]
    rec[pl.ds(shots * HIST, shots * STEPS), :] = records.astype(BF16)
    run(
        [pltpu.make_async_copy(rec, rec_out.at[g], out_sems.at[g]) for g in range(8)]
        + [pltpu.make_async_copy(cur.at[:, MID, YMID], next_out, out_sems.at[9])]
    )
    last.wait()


def stencil(cur, prv, spd, corners, rows_hot, lanes_hot, history):
    shots = cur.shape[0]
    points = rows_hot.shape[0]
    return pl.pallas_call(
        stencil_kernel,
        out_shape=(
            jax.ShapeDtypeStruct((8, shots * (HIST + STEPS), points), BF16),
            jax.ShapeDtypeStruct((shots, TILE, TILE, DEPTH), F32),
            jax.ShapeDtypeStruct((shots, TILE, TILE, DEPTH), F32),
            jax.ShapeDtypeStruct(cur.shape, F32),
            jax.ShapeDtypeStruct(cur.shape, F32),
            jax.ShapeDtypeStruct(spd.shape, F32),
        ),
        in_specs=[VMEM] * 3 + [ANY] * 4 + [VMEM] * 3,
        out_specs=(HBM,) * 3 + (VMEM,) * 3,
        input_output_aliases={0: 3, 1: 4, 2: 5},
        scratch_shapes=[
            pltpu.VMEM((shots * (HIST + STEPS), points), BF16),
            pltpu.SemaphoreType.DMA((12,)),
            pltpu.SemaphoreType.DMA((10,)),
        ],
        compiler_params=pltpu.CompilerParams(vmem_limit_bytes=20 << 20),
        cost_estimate=pl.CostEstimate(flops=2_000_000_000, bytes_accessed=12_000_000, transcendentals=0),
        name="stencil",
    )(cur, prv, spd, *corners, rows_hot, lanes_hot, history)


def columns_kernel(delay, records, green, out):
    groups, rows, _ = records.shape
    rows = rows // 2
    half = rows // 2
    lags = green.shape[0]
    width = green.shape[2]
    sel_row = lax.broadcasted_iota(jnp.int32, (half, 2 * rows), 0)
    sel_col = lax.broadcasted_iota(jnp.int32, (half, 2 * rows), 1)
    col_shot = (sel_col % rows) // STEPS
    col_time = (sel_col // rows) * HIST + sel_col % STEPS
    both = [records[g] for g in range(groups)]
    parts = []
    for h in range(2):
        row_shot = sel_row // STEPS + h * (half // STEPS)
        total = None
        for lag in range(lags):
            wanted = HIST + sel_row % STEPS - delay[lag]
            sel = jnp.logical_and(col_shot == row_shot, col_time == wanted)
            sel = sel.astype(F32).astype(BF16)
            window = jnp.concatenate(
                [jnp.dot(sel, b, preferred_element_type=F32).astype(BF16) for b in both], axis=0
            )
            term = jnp.dot(window, green[lag], preferred_element_type=F32)
            total = term if total is None else total + term
        parts.append(total)
    lane = lax.broadcasted_iota(jnp.int32, (groups * half, 128), 1)
    for m in range(width // 128):
        a = parts[0][:, m * 128 : (m + 1) * 128]
        b = parts[1][:, m * 128 : (m + 1) * 128]
        out[2 * m] = jnp.where(lane < 64, a, pltpu.roll(b, 64, 1)).astype(BF16)
        out[2 * m + 1] = jnp.where(lane < 64, pltpu.roll(a, 64, 1), b).astype(BF16)


def columns(delay, records, green):
    vmem = pl.BlockSpec(memory_space=pltpu.VMEM)
    return pl.pallas_call(
        columns_kernel,
        out_shape=jax.ShapeDtypeStruct((16, 128, 128), BF16),
        in_specs=[pl.BlockSpec(memory_space=pltpu.SMEM), vmem, vmem],
        out_specs=vmem,
        compiler_params=pltpu.CompilerParams(vmem_limit_bytes=12 << 20),
        cost_estimate=pl.CostEstimate(flops=1_000_000_000, bytes_accessed=4_000_000, transcendentals=0),
        name="columns",
    )(delay, records, green)


def inject_kernel(em, cells, weights, field, wave_out, emission_out, rhs_high, rhs_low, acc, emission):
    shots = field.shape[0]
    points = cells.shape[1]
    lane = lax.broadcasted_iota(jnp.int32, (16, 128), 1)
    for tile in range(4):
        even, odd = em[2 * tile], em[2 * tile + 1]
        emission[pl.ds(0, 16), pl.ds(tile * 128, 128)] = jnp.where(lane < 64, even, pltpu.roll(odd, 64, 1))
        emission[pl.ds(16, 16), pl.ds(tile * 128, 128)] = jnp.where(lane < 64, pltpu.roll(even, 64, 1), odd)

    acc[...] = jnp.zeros_like(acc)
    row_iota = lax.broadcasted_iota(jnp.int32, (TILE * TILE, points), 0)
    lane_iota = lax.broadcasted_iota(jnp.int32, (DEPTH, points), 0)

    def body(k, carry):
        cell = cells[pl.ds(k, 1), :]
        weight = weights[pl.ds(k, 1), :]
        rows_hot = (row_iota == lax.shift_right_logical(cell, 7)).astype(F32).astype(BF16)
        lane_hot = lane_iota == jnp.bitwise_and(cell, DEPTH - 1)
        for s in range(shots):
            value = weight * emission[pl.ds(s * STEPS + STEPS - 1, 1), :]
            top = value.astype(BF16).astype(F32)
            rest = value - top
            rhs_high[pl.ds(s * DEPTH, DEPTH), :] = jnp.where(lane_hot, top, 0.0).astype(BF16)
            rhs_low[pl.ds(s * DEPTH, DEPTH), :] = jnp.where(lane_hot, rest, 0.0).astype(BF16)
        acc[...] += lax.dot_general(
            rows_hot, rhs_high[...], NT, preferred_element_type=F32
        ) + lax.dot_general(rows_hot, rhs_low[...], NT, preferred_element_type=F32)
        return carry

    lax.fori_loop(0, cells.shape[0], body, 0, unroll=4)
    for row in range(shots * STEPS):
        emission_out[row] = emission[pl.ds(row, 1), :]
    for s in range(shots):
        wave_out[s] = field[s] + acc[:, s * DEPTH : (s + 1) * DEPTH].reshape(TILE, TILE, DEPTH)


def inject(em, cells, weights, field):
    shots = field.shape[0]
    points = cells.shape[1]
    vmem = pl.BlockSpec(memory_space=pltpu.VMEM)
    return pl.pallas_call(
        inject_kernel,
        out_shape=(
            jax.ShapeDtypeStruct(field.shape, F32),
            jax.ShapeDtypeStruct((shots * STEPS, 1, points), F32),
        ),
        in_specs=[vmem] * 4,
        out_specs=(vmem, vmem),
        scratch_shapes=[
            pltpu.VMEM((shots * DEPTH, points), BF16),
            pltpu.VMEM((shots * DEPTH, points), BF16),
            pltpu.VMEM((TILE * TILE, shots * DEPTH), F32),
            pltpu.VMEM((shots * STEPS, points), F32),
        ],
        compiler_params=pltpu.CompilerParams(vmem_limit_bytes=12 << 20),
        cost_estimate=pl.CostEstimate(flops=4_000_000_000, bytes_accessed=4_000_000, transcendentals=0),
        name="inject",
    )(em, cells, weights, field)


def pack_kernel(now, prev, speed, xtail, ytail, xhead, yhead, field, sems):
    shots = now.shape[0]
    copies = [
        pltpu.make_async_copy(now, field.at[pl.ds(0, shots)], sems.at[0]),
        pltpu.make_async_copy(prev, field.at[pl.ds(shots, shots)], sems.at[1]),
        pltpu.make_async_copy(speed, field.at[2 * shots], sems.at[2]),
    ]
    for copy in copies:
        copy.start()
    for copy in copies:
        copy.wait()
    head, tail = slice(0, BAND), slice(TILE - BAND, TILE)
    xtail[...] = field[:, tail]
    ytail[...] = field[:, :, tail]
    xhead[...] = field[:, head]
    yhead[...] = field[:, :, head]


def packed(now, prev, speed):
    fields = 2 * now.shape[0] + 1
    vmem = pl.BlockSpec(memory_space=pltpu.VMEM)
    across = jax.ShapeDtypeStruct((fields, BAND, TILE, DEPTH), F32)
    along = jax.ShapeDtypeStruct((fields, TILE, BAND, DEPTH), F32)
    return pl.pallas_call(
        pack_kernel,
        out_shape=(across, along, across, along),
        in_specs=[pl.BlockSpec(memory_space=pltpu.HBM)] * 3,
        out_specs=(vmem,) * 4,
        scratch_shapes=[
            pltpu.VMEM((fields, TILE, TILE, DEPTH), F32),
            pltpu.SemaphoreType.DMA((3,)),
        ],
        compiler_params=pltpu.CompilerParams(vmem_limit_bytes=8 << 20),
        cost_estimate=pl.CostEstimate(flops=0, bytes_accessed=4_000_000, transcendentals=0),
        name="pack",
    )(*in_hbm(now, prev, speed))


def halo_blocks(now, prev, speed):
    xtail, ytail, xhead, yhead = packed(now, prev, speed)
    head, tail = slice(0, BAND), slice(TILE - BAND, TILE)
    xm = lax.ppermute(xtail, "tx", UP)
    ym = lax.ppermute(ytail, "ty", UP)
    xp = lax.ppermute(xhead, "tx", DOWN)
    yp = lax.ppermute(yhead, "ty", DOWN)
    cmm = lax.ppermute(ym[:, tail], "tx", UP)
    cpm = lax.ppermute(xp[:, :, tail], "ty", UP)
    cpp = lax.ppermute(yp[:, head], "tx", DOWN)
    cmp = lax.ppermute(xm[:, :, head], "ty", DOWN)
    return xm, xp, ym, yp, cmm, cmp, cpm, cpp


def order_kernel(place, own_in, pair_in, core_in, diag_in, out, own, pair, core, diag, sems):
    copies = [
        pltpu.make_async_copy(src, dst, sems.at[i])
        for i, (src, dst) in enumerate(
            ((own_in, own), (pair_in, pair), (core_in, core), (diag_in, diag))
        )
    ]
    for copy in copies:
        copy.start()
    for copy in copies:
        copy.wait()
    lags, _, width = own.shape
    source = lax.broadcasted_iota(jnp.int32, (256, 512), 0)
    target = lax.broadcasted_iota(jnp.int32, (256, 512), 1)
    local = source % 128
    other_row = source // 128
    for lag in range(lags):
        for m in range(width // 128):
            cut = pl.ds(m * 128, 128)
            total = None
            for other_core, (a, b) in enumerate(((own, pair), (core, diag))):
                spot = (
                    (local // 16) * 64
                    + jnp.bitwise_xor(other_row, place[0]) * 32
                    + jnp.bitwise_xor(other_core, place[1]) * 16
                    + local % 16
                )
                hot = (spot == target).astype(F32).astype(BF16)
                both = jnp.concatenate([a[lag, :, cut], b[lag, :, cut]], axis=1)
                term = jnp.dot(both, hot, preferred_element_type=F32)
                total = term if total is None else total + term
            out[lag, :, pl.ds(m * 512, 512)] = total.astype(BF16)


def gathered_green(green):
    def moved(block, pairs):
        return lax.ppermute(block, "shot", pairs)

    pair = moved(green, PAIR_SWAP)
    core = moved(green, CORE_SWAP)
    diag = moved(pair, CORE_SWAP)
    me = lax.axis_index("shot")
    place = jnp.stack([me // 2 % 2, me % 2]).astype(jnp.int32)
    lags, points, width = green.shape
    vmem = pl.BlockSpec(memory_space=pltpu.VMEM)
    return pl.pallas_call(
        order_kernel,
        out_shape=jax.ShapeDtypeStruct((lags, points, 4 * width), BF16),
        in_specs=[pl.BlockSpec(memory_space=pltpu.SMEM)]
        + [pl.BlockSpec(memory_space=pltpu.HBM)] * 4,
        out_specs=vmem,
        scratch_shapes=[pltpu.VMEM(green.shape, BF16)] * 4 + [pltpu.SemaphoreType.DMA((4,))],
        compiler_params=pltpu.CompilerParams(vmem_limit_bytes=12 << 20),
        cost_estimate=pl.CostEstimate(flops=1_000_000_000, bytes_accessed=4_000_000, transcendentals=0),
        name="order",
    )(place, *in_hbm(green, pair, core, diag))


def block(
    wave_now, wave_prev, courant, rec_index, rec_history, green, lag_delay, emit_cells, emit_weights
):
    shots = wave_now.shape[0]
    receivers = rec_index.reshape(-1)
    rows_hot = (
        lax.shift_right_logical(receivers, 7)[:, None] == jnp.arange(TILE * TILE)[None, :]
    ).astype(BF16)
    lanes_hot = (
        jnp.bitwise_and(receivers, DEPTH - 1)[:, None] == jnp.arange(DEPTH)[None, :]
    ).astype(F32)
    halos = halo_blocks(wave_now, wave_prev, courant)
    wide_green = gathered_green(green)
    band = assemble(wave_now, wave_prev, courant, halos[:4])
    records, field, wave_last = stencil(
        *band, halos[4:], rows_hot, lanes_hot, rec_history.reshape(shots * HIST, -1)
    )[:3]
    records = row_exchange(records)
    partial = columns(lag_delay, records, wide_green)
    partial = lax.all_to_all(partial, ("tx", "ty"), 0, 0, tiled=True)
    summed = jnp.sum(partial.astype(F32), axis=0)
    em = row_exchange(summed.reshape(8, 16, 128))
    wave_out, emission = inject(
        em, emit_cells.reshape(emit_cells.shape[-2:]), emit_weights.reshape(emit_weights.shape[-2:]), field
    )
    return wave_out, wave_last, emission.reshape(shots, STEPS, 1, 1, -1)


def solution(mesh):
    return jax.shard_map(
        block,
        mesh=mesh,
        in_specs=(
            P("shot", "tx", "ty", None),
            P("shot", "tx", "ty", None),
            P("tx", "ty", None),
            P("tx", "ty", None),
            P("shot", None, "tx", "ty", None),
            P(None, ("tx", "ty"), "shot"),
            P(),
            P("tx", "ty", None, None),
            P("tx", "ty", None, None),
        ),
        out_specs=(
            P("shot", "tx", "ty", None),
            P("shot", "tx", "ty", None),
            P("shot", None, "tx", "ty", None),
        ),
        check_vma=False,
    )
```
